256 devices in a mesh: trow: 16 (over x, y), tcol: 8 (over z), rep: 2 (over core).
Axes of the slice: x: 4, y: 4, z: 8, core: 2. Of those that a mesh axis runs over, the one named last changes fastest.
Arguments:
- users: float32 [131072, 128], P(('trow', 'tcol'))
- items: float32 [65536, 128], P(('tcol', 'trow'))
- ratings: bfloat16 [16, 8, 2, 64, 128, 128], P('trow', 'tcol', 'rep'), may hold values from -6 to 6
- row_mask: int32 [16, 8, 2, 64, 128], P('trow', 'tcol', 'rep'), may hold values 0 or 1
- col_mask: int32 [16, 8, 2, 64, 128], P('trow', 'tcol', 'rep'), may hold values 0 or 1
- row_slots: int32 [16, 8, 2, 64], P('trow', 'tcol', 'rep'), may hold values from 0 to 31, as said below
- col_slots: int32 [16, 8, 2, 64], P('trow', 'tcol', 'rep'), may hold values from 0 to 31, as said below
- send_users: int32 [16, 8, 2, 8, 4], P('trow', 'tcol', 'rep'), may hold values from 0 to 7, as said below
- send_items: int32 [16, 8, 2, 16, 2], P('trow', 'tcol', 'rep'), may hold values from 0 to 3, as said below
Outputs:
- users_out: float32 [131072, 128], P(('trow', 'tcol'))
- items_out: float32 [65536, 128], P(('tcol', 'trow'))
The draws below stay inside these ranges and needn't reach their ends.
Inputs may be any that keep to these rules, and one draw needn't show every extreme that they name: `send_users`: distinct within each row of the last dimension. `send_items`: distinct within each row of the last dimension. `row_slots`: every slot is named by some tile of each device. `col_slots`: every slot is named by some tile of each device.
All inputs are finite; a program needn't handle non-finite values. No bound on the sum of `row_mask` or of `col_mask` on one device may be relied on, other than what follows from the above.
Results may differ from the reference program's by a relative error of at most 0.02.
Values may be sent and summed in bfloat16 or wider, within the bound.
A program may use at most 64 MiB of HBM per device.

```python
import jax
import jax.numpy as jnp
from jax import lax

R = 128
TILE = 128
LT = 8
RT = 4
NT = 64
CAPL = 4
CAPR = 2
ITERS = 2
USERS = 131072
ITEMS = 65536
N_TROW = 16
N_TCOL = 8
N_REP = 2


def distinct_order(key, shape):
    count = shape[-1]
    scores = jax.random.randint(key, shape, 0, 1 << 20) * count + lax.broadcasted_iota(jnp.int32, shape, len(shape) - 1)
    return jnp.argsort(scores, axis=-1, stable=True).astype(jnp.int32)


def slot_list(key, lead, total):
    covering = distinct_order(jax.random.fold_in(key, 1), lead + (total,))
    others = jax.random.randint(jax.random.fold_in(key, 2), lead + (NT - total,), 0, total).astype(jnp.int32)
    joined = jnp.concatenate([covering, others], axis=-1)
    order = distinct_order(jax.random.fold_in(key, 3), lead + (NT,))
    return jnp.take_along_axis(joined, order, axis=-1)


def draw_send_users(key, part):
    lead = (N_TROW, N_TCOL, N_REP)
    return distinct_order(jax.random.fold_in(key, 11), lead + (N_TCOL, LT))[..., :CAPL]


def draw_send_items(key, part):
    lead = (N_TROW, N_TCOL, N_REP)
    return distinct_order(jax.random.fold_in(key, 12), lead + (N_TROW, RT))[..., :CAPR]


def draw_row_slots(key, part):
    return slot_list(jax.random.fold_in(key, 13), (N_TROW, N_TCOL, N_REP), N_TCOL * CAPL)


def draw_col_slots(key, part):
    return slot_list(jax.random.fold_in(key, 14), (N_TROW, N_TCOL, N_REP), N_TROW * CAPR)


def factor_draw(key, count):
    base = jax.random.normal(jax.random.fold_in(key, 1), (count, R), jnp.float32)
    col_scale = jnp.exp(jax.random.uniform(jax.random.fold_in(key, 2), (1, R), jnp.float32, -1.89712, -0.79851))
    shared = jax.random.normal(jax.random.fold_in(key, 3), (count, 1), jnp.float32)
    pattern = jax.random.normal(jax.random.fold_in(key, 5), (1, R), jnp.float32)
    return (base * col_scale + 0.15 * shared * pattern).astype(jnp.float32)


def draw_users(key, part):
    return factor_draw(jax.random.fold_in(key, 21), USERS)


def draw_items(key, part):
    return factor_draw(jax.random.fold_in(key, 22), ITEMS)


def place_ends(array, key, low, largest):
    dims = array.shape
    place = [jax.random.randint(jax.random.fold_in(key, axis), (), 0, dims[axis]) for axis in range(len(dims))]
    array = array.at[tuple(place)].set(low)
    longest = dims.index(max(dims))
    place[longest] = (place[longest] + 1) % dims[longest]
    return array.at[tuple(place)].set(largest)


def levels(key, extent, pieces, smallest, largest):
    def one(axis_at, blocks):
        draws = jax.random.uniform(jax.random.fold_in(jax.random.fold_in(key, 6), axis_at), (blocks,), jnp.float32, smallest / len(pieces), largest / len(pieces))
        return jnp.repeat(jnp.exp(draws), extent[axis_at] // blocks).reshape((-1,) + (1,) * (len(extent) - axis_at - 1))

    loudness = one(*pieces[0])
    for cut in pieces[1:]:
        loudness = loudness * one(*cut)
    return loudness


def gaussian(own_key, shape, width, bound, split=(), kind=jnp.bfloat16):
    loudness = levels(own_key, shape, split, -0.22, 0.18) if split else 1.0
    values = jax.random.normal(own_key, shape, jnp.float32) * width * loudness
    return jnp.minimum(jnp.maximum(values, -bound), bound).astype(kind)


def setup_inputs(seed: int = 0) -> dict:
    streams_of = jax.random.split(jax.random.key(seed), 10)
    users = draw_users(jax.random.fold_in(streams_of[9], 71), 0)
    items = draw_items(jax.random.fold_in(streams_of[9], 71), 0)
    ratings = gaussian(streams_of[2], (N_TROW, N_TCOL, N_REP, NT, TILE, TILE), 1.0, 6.0, ((0, 16), (1, 8), (2, 2)))
    row_mask = place_ends((jax.random.randint(streams_of[3], (N_TROW, N_TCOL, N_REP, NT, TILE), 0, 4) < 3).astype(jnp.int32), jax.random.fold_in(streams_of[3], 1), 0, 1)
    col_mask = place_ends((jax.random.randint(streams_of[4], (N_TROW, N_TCOL, N_REP, NT, TILE), 0, 4) < 3).astype(jnp.int32), jax.random.fold_in(streams_of[4], 1), 0, 1)
    row_slots = draw_row_slots(jax.random.fold_in(streams_of[9], 71), 0)
    col_slots = draw_col_slots(jax.random.fold_in(streams_of[9], 71), 0)
    send_users = draw_send_users(jax.random.fold_in(streams_of[9], 71), 0)
    send_items = draw_send_items(jax.random.fold_in(streams_of[9], 71), 0)
    return {"users": users, "items": items, "ratings": ratings, "row_mask": row_mask, "col_mask": col_mask, "row_slots": row_slots, "col_slots": col_slots, "send_users": send_users, "send_items": send_items}


def precondition(gradient, gramian):
    factor = jnp.linalg.cholesky(gramian)
    return jax.scipy.linalg.cho_solve((factor, True), gradient.T).T

def reference(users, items, ratings, row_mask, col_mask, row_slots, col_slots, send_users, send_items):
    blocks = N_TROW * N_TCOL * N_REP
    first = jnp.arange(N_TROW, dtype=jnp.int32).reshape(-1, 1, 1, 1)
    second = jnp.arange(N_TCOL, dtype=jnp.int32).reshape(1, -1, 1, 1)
    third = jnp.arange(N_REP, dtype=jnp.int32).reshape(1, 1, -1, 1)
    source_u = (row_slots // CAPL).astype(jnp.int32)
    tile_rows = source_u * LT + send_users[first, source_u, third, second, (row_slots % CAPL).astype(jnp.int32)]
    source_i = (col_slots // CAPR).astype(jnp.int32)
    tile_cols = source_i * RT + send_items[source_i, second, third, first, (col_slots % CAPR).astype(jnp.int32)]
    global_rows = (first * (LT * N_TCOL) + tile_rows).reshape(blocks, NT).astype(jnp.int32)
    global_cols = (second * (RT * N_TROW) + tile_cols).reshape(blocks, NT).astype(jnp.int32)
    ratings_all = ratings.reshape(blocks, NT, TILE, TILE)
    rows_all = row_mask.reshape(blocks, NT, TILE)
    cols_all = col_mask.reshape(blocks, NT, TILE)
    user_coef = 2.0 * ITEMS * LT / (TILE * NT * N_REP)
    item_coef = 2.0 * USERS * RT / (TILE * NT * N_REP)
    for iteration in range(ITERS):
        gram_users = jnp.dot(users.T.astype(jnp.float32), users.astype(jnp.float32), precision=lax.Precision.HIGHEST, preferred_element_type=jnp.float32)
        gram_items = jnp.dot(items.T.astype(jnp.float32), items.astype(jnp.float32), precision=lax.Precision.HIGHEST, preferred_element_type=jnp.float32)
        user_half = users.astype(jnp.bfloat16).reshape(-1, TILE, R)
        item_half = items.astype(jnp.bfloat16).reshape(-1, TILE, R)

        def visit(block, carry):
            acc_users, acc_items = carry
            rows = global_rows[block]
            cols = global_cols[block]
            x_tiles = user_half[rows].astype(jnp.float32)
            y_tiles = item_half[cols].astype(jnp.float32)
            predicted = jnp.einsum('tar,tbr->tab', x_tiles, y_tiles)
            weights = (rows_all[block][:, :, None] * cols_all[block][:, None, :]).astype(jnp.float32)
            errors = (weights * (predicted - ratings_all[block].astype(jnp.float32))).astype(jnp.bfloat16)
            errors = lax.optimization_barrier(errors).astype(jnp.float32)
            acc_users = acc_users.at[rows].add(jnp.einsum('tab,tbr->tar', errors, y_tiles))
            acc_items = acc_items.at[cols].add(jnp.einsum('tab,tar->tbr', errors, x_tiles))
            return (acc_users, acc_items)
        start = (jnp.zeros((USERS // TILE, TILE, R), jnp.float32), jnp.zeros((ITEMS // TILE, TILE, R), jnp.float32))
        grad_users, grad_items = lax.fori_loop(0, blocks, visit, start)
        new_users = users - user_coef * precondition(grad_users.reshape(-1, R), gram_items)
        new_items = items - item_coef * precondition(grad_items.reshape(-1, R), gram_users)
        users, items = (new_users, new_items)
    return (users, items)
```

```python
import functools

import jax
import jax.numpy as jnp
from jax import lax
from jax.experimental import pallas as pl
from jax.experimental.pallas import tpu as pltpu
from jax.sharding import PartitionSpec as P

ITERS = 2
TILE = 128
NX = 4
NY = 4
NZ = 8
NXY = NX * NY
LT = 8
RT = 4
NT = 64
CAPL = 4
CAPR = 2
HU = LT // 2
HI = RT // 2
F32 = jnp.float32
BF16 = jnp.bfloat16
HIGHEST = lax.Precision.HIGHEST


def kernel(
    user_coef,
    item_coef,
    tab,
    sends,
    row_mask,
    col_mask,
    users,
    items,
    ratings,
    out_u,
    out_i,
    lists_u,
    lists_i,
    slists_u,
    slists_i,
    x_row,
    y_row,
    x_col,
    tab_u,
    flag_u,
    tab_i,
    flag_i,
    u_cur,
    i_cur,
    rat,
    weights,
    pool_u,
    pool_i,
    errs,
    run_u,
    run_i,
    gmine,
    gsend,
    gsib,
    gz,
    gchunk,
    gxy,
    gsum,
    gfull,
    gother,
    sibs_u,
    sibr_u,
    ring_s,
    ring_r,
    sibs_i,
    sibr_i,
    half_s,
    half_r,
    full_s,
    full_r,
    quarter,
    ah_s,
    ah_r,
    af_s,
    af_r,
    ssem,
    rsem,
    lsem,
):
    trow = lax.axis_index("trow")
    z = lax.axis_index("tcol")
    c = lax.axis_index("rep")
    other = 1 - c
    x = trow // NY
    y = trow % NY
    a = jnp.where(c == 0, x, y)
    b = jnp.where(c == 0, y, x)
    sa = 4 - 3 * c
    sb = 1 + 3 * c

    def cell(oa, ob):
        return ((a + oa) % 4) * sa + ((b + ob) % 4) * sb

    def remote(src, dst, send_sem, recv_sem, where):
        return pltpu.make_async_remote_copy(
            src_ref=src,
            dst_ref=dst,
            send_sem=send_sem,
            recv_sem=recv_sem,
            device_id=where,
            device_id_type=pl.DeviceIdType.MESH,
        )

    def await_bytes(ref, sem):
        pltpu.make_async_copy(ref, ref, sem).wait()

    sibling = {"rep": other}

    load_r = pltpu.make_async_copy(ratings, rat, lsem.at[0])
    load_u = pltpu.make_async_copy(users.at[pl.ds(HU * c, HU)], u_cur, lsem.at[1])
    load_i = pltpu.make_async_copy(items.at[pl.ds(HI * c, HI)], i_cur, lsem.at[2])
    load_u.start()
    load_i.start()
    load_r.start()

    barrier = pltpu.get_barrier_semaphore()
    for d in range(1, NZ):
        pl.semaphore_signal(
            barrier, inc=1, device_id={"tcol": (z + d) % NZ}, device_id_type=pl.DeviceIdType.MESH
        )
    for d in range(1, NXY):
        pl.semaphore_signal(
            barrier,
            inc=1,
            device_id={"trow": (trow + d) % NXY},
            device_id_type=pl.DeviceIdType.MESH,
        )
    pl.semaphore_signal(barrier, inc=1, device_id=sibling, device_id_type=pl.DeviceIdType.MESH)
    pl.semaphore_wait(barrier, NZ - 1 + NXY - 1 + 1)

    for d in range(1, NZ):
        remote(
            sends.at[0], lists_u.at[z], lsem.at[3], lsem.at[4], {"tcol": (z + d) % NZ}
        ).start()
    for d in range(1, NXY):
        remote(
            sends.at[0], lists_i.at[trow], lsem.at[5], lsem.at[6], {"trow": (trow + d) % NXY}
        ).start()
    lists_u[z] = sends[0]
    lists_i[trow] = sends[0]
    load_u.wait()
    load_i.wait()

    lane = lax.broadcasted_iota(jnp.int32, (TILE, TILE), 1)

    def make_weights():
        padded = jnp.concatenate(
            [row_mask[...].astype(F32), jnp.zeros((TILE - NT, TILE), F32)], axis=0
        )
        quarter[0, 0] = padded.T

        def one(t, carry):
            spread = jnp.take_along_axis(
                quarter[0, 0], jnp.full((TILE, TILE), t, jnp.int32), axis=1, mode="promise_in_bounds"
            )
            weights[t] = (spread * col_mask[pl.ds(t, 1), :].astype(F32)).astype(BF16)
            return carry

        lax.fori_loop(0, NT, one, 0)

    def make_tables():
        await_bytes(lists_u.at[pl.ds(0, NZ - 1)], lsem.at[3])
        await_bytes(lists_u.at[pl.ds(0, NZ - 1)], lsem.at[4])
        await_bytes(lists_i.at[pl.ds(0, NXY - 1)], lsem.at[5])
        await_bytes(lists_i.at[pl.ds(0, NXY - 1)], lsem.at[6])
        down_u = pltpu.make_async_copy(lists_u, slists_u, lsem.at[7])
        down_i = pltpu.make_async_copy(lists_i, slists_i, lsem.at[8])
        down_u.start()
        down_i.start()
        down_u.wait()
        down_i.wait()

        def user_tile(slot):
            source = slot // CAPL
            return source * LT + slists_u[source, 0, z * CAPL + slot % CAPL]

        def item_tile(slot):
            source = slot // CAPR
            return source * RT + slists_i[source, 0, NZ * CAPL + trow * CAPR + slot % CAPR]

        def one(k, carry):
            x_row[k] = user_tile(tab[1, k])
            y_row[k] = item_tile(tab[2, k])
            x_col[k] = user_tile(tab[5, k])
            source = k // LT
            found = jnp.int32(-1)
            for s in range(CAPL):
                found = jnp.where(
                    slists_u[source, 0, z * CAPL + s] == k % LT, tab[6, source * CAPL + s], found
                )
            flag_u[k] = jnp.where(found >= 0, 1, 0)
            tab_u[k] = jnp.maximum(found, 0)
            source = k // RT
            found = jnp.int32(-1)
            for s in range(CAPR):
                found = jnp.where(
                    slists_i[source, 0, NZ * CAPL + trow * CAPR + s] == k % RT,
                    tab[7, source * CAPR + s],
                    found,
                )
            flag_i[k] = jnp.where(found >= 0, 1, 0)
            tab_i[k] = jnp.maximum(found, 0)
            return carry

        lax.fori_loop(0, NT, one, 0)

    def iteration(it, carry):
        names = {}
        pending = []

        def number(name):
            names.setdefault(name, len(names))
            return names[name]

        def begin(name, src, dst, where):
            n = number(name)
            copy = remote(src, dst, ssem.at[n], rsem.at[it, n], where)
            copy.start()
            pending.append(copy)

        def arrive(name, ref):
            await_bytes(ref, rsem.at[it, number(name)])

        for l in range(HU):
            pool_u[it, z * LT + HU * c + l] = u_cur[l].astype(BF16)
        for l in range(HI):
            pool_i[it, trow * RT + HI * c + l] = i_cur[l].astype(BF16)

        def pair_u(o, pr):
            return pool_u.at[it, pl.ds(((z + o) % NZ) * LT + HU * c + 2 * pr, 2)]

        def send_u(way, step, pr):
            ref = pair_u(-way * (step - 1) + NZ, pr)
            begin(("u", way, step, pr), ref, ref, {"tcol": (z + way + NZ) % NZ})

        def sib_u(o, pr):
            ref = pair_u(o, pr)
            remote(ref, ref, ssem.at[number("su")], rsem.at[it, number("su")], sibling).start()

        def chunk_i(oa, ob):
            return pool_i.at[it, pl.ds(cell(oa, ob) * RT + HI * c, HI)]

        def tile_i(oa, ob, j):
            return pool_i.at[it, pl.ds(cell(oa, ob) * RT + HI * c + j, 1)]

        def along_a(way):
            return {"trow": cell(way + 4, 0)}

        def along_b(way):
            return {"trow": cell(0, way + 4)}

        def sib_i(oa, ob):
            ref = chunk_i(oa, ob)
            remote(ref, ref, ssem.at[number("si")], rsem.at[it, number("si")], sibling).start()

        def second_i(oa):
            for way in (1, -1):
                begin(("b", way, oa), chunk_i(oa, 0), chunk_i(oa, 0), along_b(way))

        for pr in range(2):
            for way in (1, -1):
                send_u(way, 1, pr)
        for way in (1, -1):
            begin(("a", way), chunk_i(0, 0), chunk_i(0, 0), along_a(way))
        second_i(0)
        for pr in range(2):
            sib_u(0, pr)
        sib_i(0, 0)

        def gram(ref, count):
            flat = ref[...].reshape(count * TILE, TILE)
            return lax.dot_general(
                flat, flat, (((0,), (0,)), ((), ())), precision=HIGHEST, preferred_element_type=F32
            )

        gram_u = gram(u_cur, HU)
        gram_i = gram(i_cur, HI)
        gsend[...] = jnp.where(c == 0, gram_i, gram_u)
        begin("gs", gsend, gsib.at[it], sibling)
        gmine[...] = jnp.where(c == 0, gram_u, gram_i)

        @pl.when(it == 0)
        def _():
            make_weights()

        arrive("gs", gsib.at[it])
        gmine[...] += gsib[it]
        for d in range(1, NZ):
            zz = (z + d) % NZ
            remote(
                gmine.at[pl.ds(16 * zz, 16)],
                gz.at[it, d - 1],
                ssem.at[number("gz")],
                rsem.at[it, number("gz")],
                {"tcol": zz},
            ).start()

        def got_u(way, step, pr):
            arrive(("u", way, step, pr), pair_u(-way * step + NZ, pr))
            if step < 3 or (step == 3 and pr == (0 if way == 1 else 1)):
                send_u(way, step + 1, pr)
            sib_u(-way * step + NZ, pr)

        def first_got(way):
            oa = (4 - way) % 4
            arrive(("a", way), chunk_i(oa, 0))
            j = 0 if way == 1 else 1
            ref = tile_i(oa, 0, j)
            begin(("af", way), ref, ref, along_a(way))
            second_i(oa)
            sib_i(oa, 0)

        def first_far():
            for way, j in ((1, 0), (-1, 1)):
                arrive(("af", way), tile_i(2, 0, j))
            second_i(2)
            sib_i(2, 0)

        def second_got(oa):
            for way, j in ((1, 0), (-1, 1)):
                arrive(("b", way, oa), chunk_i(oa, 4 - way))
                ref = tile_i(oa, 4 - way, j)
                begin(("bf", way, oa), ref, ref, along_b(way))
                sib_i(oa, 4 - way)

        def second_far(oa):
            for way, j in ((1, 0), (-1, 1)):
                arrive(("bf", way, oa), tile_i(oa, 2, j))
            sib_i(oa, 2)

        for pr in range(2):
            for way in (1, -1):
                got_u(way, 1, pr)
        first_got(1)
        first_got(-1)
        second_got(0)
        first_far()
        for pr in range(2):
            for way in (1, -1):
                got_u(way, 2, pr)

        await_bytes(gz.at[it], rsem.at[it, number("gz")])
        total = gmine[pl.ds(16 * z, 16), :]
        for d in range(NZ - 1):
            total = total + gz[it, d]
        gchunk[...] = total
        gxy[it, trow] = total
        for d in range(1, NXY):
            remote(
                gchunk,
                gxy.at[it, trow],
                ssem.at[number("gxy")],
                rsem.at[it, number("gxy")],
                {"trow": (trow + d) % NXY},
            ).start()

        @pl.when(it == 0)
        def _():
            make_tables()

        second_got(3)
        second_got(1)
        for way in (1, -1):
            got_u(way, 3, 0)
        second_far(0)
        for way in (1, -1):
            got_u(way, 3, 1)
        second_got(2)

        await_bytes(gxy.at[it, pl.ds(0, NXY - 1)], rsem.at[it, number("gxy")])
        total = gxy[it, 0]
        for d in range(1, NXY):
            total = total + gxy[it, d]
        gsum[...] = total
        gfull[it, pl.ds(16 * z, 16), :] = total
        for d in range(1, NZ):
            remote(
                gsum,
                gfull.at[it, pl.ds(16 * z, 16)],
                ssem.at[number("gd")],
                rsem.at[it, number("gd")],
                {"tcol": (z + d) % NZ},
            ).start()

        second_far(3)
        second_far(1)
        got_u(1, 4, 0)
        got_u(-1, 4, 1)
        second_far(2)

        @pl.when(it == 0)
        def _():
            load_r.wait()

        await_bytes(pool_u.at[it, pl.ds(0, NT // 2)], rsem.at[it, number("su")])
        await_bytes(pool_i.at[it, pl.ds(0, NT // 2)], rsem.at[it, number("si")])

        def user_pass(k, carry):
            run, before = carry
            t = tab[0, k]
            slot = tab[1, k]
            xt = pool_u[it, x_row[k]]
            yt = pool_i[it, y_row[k]]
            predicted = lax.dot_general(
                xt, yt, (((1,), (1,)), ((), ())), preferred_element_type=F32
            )
            err = ((predicted - rat[t].astype(F32)) * weights[t].astype(F32)).astype(BF16)
            errs[k] = err
            term = jnp.dot(err, yt, preferred_element_type=F32)
            run = jnp.where(slot == before, run, 0.0) + term
            run_u[k] = run
            return run, slot

        zero = jnp.zeros((TILE, TILE), F32)
        lax.fori_loop(0, NT, user_pass, (zero, jnp.int32(-1)), unroll=2)

        def own_u(o, l):
            p = ((z + o) % NZ) * LT + HU * c + l
            return run_u[tab_u[p]] * flag_u[p].astype(F32)

        def share_u(o):
            def one(l, carry):
                p = ((z + o) % NZ) * LT + HU * other + l
                sibs_u[o, l] = (run_u[tab_u[p]] * flag_u[p].astype(F32)).astype(BF16)
                return carry

            lax.fori_loop(0, HU, one, 0)
            begin(("su", o), sibs_u.at[o], sibr_u.at[it, o], sibling)

        for o in (4, 3, 5, 2, 6, 1, 7, 0):
            share_u(o)

        def item_pass(k, carry):
            run, before = carry
            slot = tab[4, k]
            term = lax.dot_general(
                errs[tab[3, k]],
                pool_u[it, x_col[k]],
                (((0,), (0,)), ((), ())),
                preferred_element_type=F32,
            )
            run = jnp.where(slot == before, run, 0.0) + term
            run_i[k] = run
            return run, slot

        def ring_send(w, k, pr):
            ref = ring_s.at[w, k, pl.ds(2 * pr, 2)]
            begin(
                ("r", w, k, pr),
                ref,
                ring_r.at[it, w, k, pl.ds(2 * pr, 2)],
                {"tcol": (z + (1, NZ - 1)[w]) % NZ},
            )

        def ring_first(w):
            for l in (2 * w, 2 * w + 1):
                ring_s[w, 0, l] = (own_u(4, l) + sibr_u[it, 4, l].astype(F32)).astype(BF16)
            ring_send(w, 0, w)

        def ring_step(w, k):
            o = (4 - k) if w == 0 else 4 + k
            arrive(("su", o), sibr_u.at[it, o])
            for pr in (w, 1 - w):
                held = k > 1 or pr == w
                if held:
                    arrive(("r", w, k - 1, pr), ring_r.at[it, w, k - 1, pl.ds(2 * pr, 2)])
                for l in (2 * pr, 2 * pr + 1):
                    value = own_u(o, l) + sibr_u[it, o, l].astype(F32)
                    if held:
                        value = value + ring_r[it, w, k - 1, l].astype(F32)
                    ring_s[w, k, l] = value.astype(BF16)
                ring_send(w, k, pr)

        arrive(("su", 4), sibr_u.at[it, 4])
        ring_first(0)
        ring_first(1)
        lax.fori_loop(0, NT, item_pass, (zero, jnp.int32(-1)), unroll=2)

        def share_i(p, carry):
            q = p * RT + HI * other
            for j in range(HI):
                sibs_i[p, j] = (run_i[tab_i[q + j]] * flag_i[q + j].astype(F32)).astype(BF16)
            return carry

        lax.fori_loop(0, NXY, share_i, 0)
        begin("shi", sibs_i, sibr_i.at[it], sibling)
        ring_step(0, 1)
        ring_step(1, 1)
        arrive("shi", sibr_i.at[it])

        def own_i(oa, ob, j):
            p = cell(oa, ob)
            q = p * RT + HI * c + j
            return run_i[tab_i[q]] * flag_i[q].astype(F32) + sibr_i[it, p, j].astype(F32)

        for w, ob in ((0, 1), (1, 3)):

            def one(o, carry, w=w):
                half_s[w, o] = own_i(o, 2, w).astype(BF16)
                return carry

            lax.fori_loop(0, 4, one, 0)
            begin(("h", w), half_s.at[w], half_r.at[it, w], {"trow": cell(0, ob)})

        await_bytes(gfull.at[it, pl.ds(0, 16 * (NZ - 1))], rsem.at[it, number("gd")])

        def eliminate(k, carry):
            mat = gfull[it]
            row = gfull[it, pl.ds(k, 1), :]
            pick = jnp.full((TILE, TILE), k, jnp.int32)
            column = jnp.take_along_axis(mat, pick, axis=1, mode="promise_in_bounds")
            pivot = gfull[it, pl.ds(k, 1), :]
            pivot = jnp.sum(jnp.where(lane[0:1] == k, pivot, 0.0), axis=1, keepdims=True)
            scaled = jnp.where(lane[0:1] == k, 1.0, row) / pivot
            gfull[it] = jnp.where(lane == k, 0.0, mat) - column * scaled
            gfull[it, pl.ds(k, 1), :] = scaled
            return carry

        def invert(low, high):
            lax.fori_loop(low, high, eliminate, 0)

        invert(0, 32)
        ring_step(0, 2)
        ring_step(1, 2)

        for w, ob in ((0, 1), (1, 3)):
            arrive(("h", w), half_r.at[it, w])

            def one(o, carry, w=w, ob=ob):
                for j in range(HI):
                    value = own_i(o, ob, j)
                    if j == w:
                        value = value + half_r[it, w, o].astype(F32)
                    full_s[w, o, j] = value.astype(BF16)
                return carry

            lax.fori_loop(0, 4, one, 0)
            begin(("f", w), full_s.at[w], full_r.at[it, w], {"trow": cell(0, ob)})

        invert(32, 64)
        ring_step(0, 3)
        ring_step(1, 3)

        for w in range(2):
            arrive(("f", w), full_r.at[it, w])

        def one(o, carry):
            for j in range(HI):
                quarter[o, j] = (
                    own_i(o, 0, j) + full_r[it, 0, o, j].astype(F32) + full_r[it, 1, o, j].astype(F32)
                )
            return carry

        lax.fori_loop(0, 4, one, 0)
        for w, oa in ((0, 1), (1, 3)):
            ah_s[w] = quarter[2, w].astype(BF16)
            begin(("ah", w), ah_s.at[w], ah_r.at[it, w], {"trow": cell(oa, 0)})

        invert(64, 96)

        for w, oa in ((0, 1), (1, 3)):
            arrive(("ah", w), ah_r.at[it, w])
            for j in range(HI):
                value = quarter[oa, j]
                if j == w:
                    value = value + ah_r[it, w].astype(F32)
                af_s[w, j] = value.astype(BF16)
            begin(("af2", w), af_s.at[w], af_r.at[it, w], {"trow": cell(oa, 0)})

        invert(96, TILE)
        begin("inv", gfull.at[it], gother.at[it], sibling)
        arrive(("su", 0), sibr_u.at[it, 0])
        for w in range(2):
            for pr in range(2):
                arrive(("r", w, 3, pr), ring_r.at[it, w, 3, pl.ds(2 * pr, 2)])
        grad_u = jnp.concatenate(
            [
                own_u(0, l)
                + sibr_u[it, 0, l].astype(F32)
                + ring_r[it, 0, 3, l].astype(F32)
                + ring_r[it, 1, 3, l].astype(F32)
                for l in range(HU)
            ],
            axis=0,
        )
        for w in range(2):
            arrive(("af2", w), af_r.at[it, w])
        grad_i = jnp.concatenate(
            [
                quarter[0, j] + af_r[it, 0, j].astype(F32) + af_r[it, 1, j].astype(F32)
                for j in range(HI)
            ],
            axis=0,
        )
        arrive("inv", gother.at[it])
        mine = gfull[it]
        theirs = gother[it]
        inverse_u = jnp.where(c == 0, mine, theirs)
        inverse_i = jnp.where(c == 0, theirs, mine)
        step_u = jnp.dot(grad_u, inverse_i, precision=HIGHEST, preferred_element_type=F32)
        step_i = jnp.dot(grad_i, inverse_u, precision=HIGHEST, preferred_element_type=F32)
        u_cur[...] = u_cur[...] - user_coef * step_u.reshape(HU, TILE, TILE)
        i_cur[...] = i_cur[...] - item_coef * step_i.reshape(HI, TILE, TILE)

        for copy in pending:
            copy.wait_send()
        await_bytes(pool_u.at[it, pl.ds(0, NT // 2)], ssem.at[number("su")])
        await_bytes(pool_i.at[it, pl.ds(0, NT // 2)], ssem.at[number("si")])
        await_bytes(gz.at[it], ssem.at[number("gz")])
        await_bytes(gxy.at[it, pl.ds(0, NXY - 1)], ssem.at[number("gxy")])
        await_bytes(gfull.at[it, pl.ds(0, 16 * (NZ - 1))], ssem.at[number("gd")])
        assert len(names) <= 128, len(names)
        return carry

    lax.fori_loop(0, ITERS, iteration, 0)

    last_u = remote(u_cur, out_u.at[pl.ds(HU * c, HU)], lsem.at[1], lsem.at[7], sibling)
    last_i = remote(i_cur, out_i.at[pl.ds(HI * c, HI)], lsem.at[2], lsem.at[8], sibling)
    last_u.start()
    last_i.start()
    for l in range(HU):
        out_u[HU * c + l] = u_cur[l]
    for l in range(HI):
        out_i[HI * c + l] = i_cur[l]
    last_u.wait()
    last_i.wait()


def slot_order(slots):
    count = slots.shape[0]
    at = lax.broadcasted_iota(jnp.int32, (count, count), 0)
    against = lax.broadcasted_iota(jnp.int32, (count, count), 1)
    mine = slots[:, None]
    theirs = slots[None, :]
    ahead = (theirs < mine) | ((theirs == mine) & (against < at))
    rank = jnp.sum(ahead.astype(jnp.int32), axis=1)
    placed = (rank[:, None] == against).astype(jnp.int32)
    return rank, placed


def on_device(
    users, items, ratings, row_mask, col_mask, row_slots, col_slots, send_users, send_items
):
    own_users = users.shape[0] // TILE
    own_items = items.shape[0] // TILE
    all_users = own_users * TILE * NXY * NZ
    all_items = own_items * TILE * NXY * NZ
    user_coef = 2.0 * all_items * own_users / (TILE * NT * 2)
    item_coef = 2.0 * all_users * own_items / (TILE * NT * 2)
    row_list = row_slots.reshape(-1)
    col_list = col_slots.reshape(-1)
    rank_r, placed_r = slot_order(row_list)
    _, placed_c = slot_order(col_list)
    numbers = jnp.arange(NT, dtype=jnp.int32)
    by_row = jnp.sum(placed_r * numbers[:, None], axis=0)
    rs = jnp.sum(placed_r * row_list[:, None], axis=0)
    rc = jnp.sum(placed_r * col_list[:, None], axis=0)
    epos = jnp.sum(placed_c * rank_r[:, None], axis=0)
    cs = jnp.sum(placed_c * col_list[:, None], axis=0)
    cr = jnp.sum(placed_c * row_list[:, None], axis=0)
    last_r = jnp.sum((row_list[:, None] <= numbers[None, :]).astype(jnp.int32), axis=0) - 1
    last_c = jnp.sum((col_list[:, None] <= numbers[None, :]).astype(jnp.int32), axis=0) - 1
    tab = jnp.stack([by_row, rs, rc, epos, cs, cr, last_r, last_c])
    sends = jnp.concatenate(
        [send_users.reshape(-1), send_items.reshape(-1), jnp.zeros((64,), jnp.int32)]
    ).reshape(1, 1, 128)

    any_spec = pl.BlockSpec(memory_space=pl.ANY)
    vmem_spec = pl.BlockSpec(memory_space=pltpu.VMEM)
    smem_spec = pl.BlockSpec(memory_space=pltpu.SMEM)
    square = (TILE, TILE)
    table = pltpu.SMEM((NT,), jnp.int32)
    out_u, out_i = pl.pallas_call(
        functools.partial(kernel, user_coef, item_coef),
        out_shape=(
            jax.ShapeDtypeStruct((LT,) + square, F32),
            jax.ShapeDtypeStruct((RT,) + square, F32),
        ),
        in_specs=[smem_spec, vmem_spec, vmem_spec, vmem_spec, any_spec, any_spec, any_spec],
        out_specs=(vmem_spec, vmem_spec),
        scratch_shapes=[
            pltpu.VMEM((NZ, 1, 128), jnp.int32),
            pltpu.VMEM((NXY, 1, 128), jnp.int32),
            pltpu.SMEM((NZ, 1, 128), jnp.int32),
            pltpu.SMEM((NXY, 1, 128), jnp.int32),
            table,
            table,
            table,
            table,
            table,
            table,
            table,
            pltpu.VMEM((HU,) + square, F32),
            pltpu.VMEM((HI,) + square, F32),
            pltpu.VMEM((NT,) + square, BF16),
            pltpu.VMEM((NT,) + square, BF16),
            pltpu.VMEM((ITERS, NT) + square, BF16),
            pltpu.VMEM((ITERS, NT) + square, BF16),
            pltpu.VMEM((NT,) + square, BF16),
            pltpu.VMEM((NT,) + square, F32),
            pltpu.VMEM((NT,) + square, F32),
            pltpu.VMEM(square, F32),
            pltpu.VMEM(square, F32),
            pltpu.VMEM((ITERS,) + square, F32),
            pltpu.VMEM((ITERS, NZ - 1, 16, TILE), F32),
            pltpu.VMEM((16, TILE), F32),
            pltpu.VMEM((ITERS, NXY, 16, TILE), F32),
            pltpu.VMEM((16, TILE), F32),
            pltpu.VMEM((ITERS,) + square, F32),
            pltpu.VMEM((ITERS,) + square, F32),
            pltpu.VMEM((NZ, HU) + square, BF16),
            pltpu.VMEM((ITERS, NZ, HU) + square, BF16),
            pltpu.VMEM((2, 4, HU) + square, BF16),
            pltpu.VMEM((ITERS, 2, 4, HU) + square, BF16),
            pltpu.VMEM((NXY, HI) + square, BF16),
            pltpu.VMEM((ITERS, NXY, HI) + square, BF16),
            pltpu.VMEM((2, 4) + square, BF16),
            pltpu.VMEM((ITERS, 2, 4) + square, BF16),
            pltpu.VMEM((2, 4, HI) + square, BF16),
            pltpu.VMEM((ITERS, 2, 4, HI) + square, BF16),
            pltpu.VMEM((4, HI) + square, F32),
            pltpu.VMEM((2,) + square, BF16),
            pltpu.VMEM((ITERS, 2) + square, BF16),
            pltpu.VMEM((2, HI) + square, BF16),
            pltpu.VMEM((ITERS, 2, HI) + square, BF16),
            pltpu.SemaphoreType.DMA((128,)),
            pltpu.SemaphoreType.DMA((ITERS, 128)),
            pltpu.SemaphoreType.DMA((9,)),
        ],
        compiler_params=pltpu.CompilerParams(
            collective_id=0, has_side_effects=True, vmem_limit_bytes=60 * 1024 * 1024
        ),
        name="scaled_gd",
    )(
        tab,
        sends,
        row_mask.reshape(NT, TILE),
        col_mask.reshape(NT, TILE),
        users.reshape((LT,) + square),
        items.reshape((RT,) + square),
        ratings.reshape((NT,) + square),
    )
    return out_u.reshape(users.shape), out_i.reshape(items.shape)


def solution(mesh):
    return jax.shard_map(
        on_device,
        mesh=mesh,
        in_specs=(
            P(("trow", "tcol"), None),
            P(("tcol", "trow"), None),
            P("trow", "tcol", "rep", None, None, None),
            P("trow", "tcol", "rep", None, None),
            P("trow", "tcol", "rep", None, None),
            P("trow", "tcol", "rep", None),
            P("trow", "tcol", "rep", None),
            P("trow", "tcol", "rep", None, None),
            P("trow", "tcol", "rep", None, None),
        ),
        out_specs=(P(("trow", "tcol"), None), P(("tcol", "trow"), None)),
        check_vma=False,
    )
```

```python
import functools

import jax
import jax.numpy as jnp
from jax import lax
from jax.experimental import pallas as pl
from jax.experimental.pallas import tpu as pltpu
from jax.sharding import PartitionSpec as P

ITERS = 2
TILE = 128
NX = 4
NY = 4
NZ = 8
NXY = NX * NY
LT = 8
RT = 4
NT = 64
CAPL = 4
CAPR = 2
HU = LT // 2
HI = RT // 2
F32 = jnp.float32
BF16 = jnp.bfloat16
HIGHEST = lax.Precision.HIGHEST


def kernel(
    user_coef,
    item_coef,
    row_slots,
    col_slots,
    sends,
    row_mask,
    col_mask,
    users,
    items,
    ratings,
    out_u,
    out_i,
    lists_u,
    lists_i,
    rows_u,
    rows_i,
    slists_u,
    slists_i,
    vtab,
    tab,
    x_row,
    y_row,
    x_col,
    tab_u,
    tab_i,
    u_cur,
    i_cur,
    rat,
    weights,
    pool_u,
    pool_i,
    errs,
    run_u,
    run_i,
    gmine,
    gsend,
    gsib,
    gz,
    gchunk,
    gxy,
    gsum,
    gfull,
    gother,
    sibs_u,
    sibr_u,
    ring_s,
    ring_r,
    sibs_i,
    sibr_i,
    half_s,
    half_r,
    full_s,
    full_r,
    quarter,
    ah_s,
    ah_r,
    af_s,
    af_r,
    ssem,
    rsem,
    lsem,
):
    trow = lax.axis_index("trow")
    z = lax.axis_index("tcol")
    c = lax.axis_index("rep")
    other = 1 - c
    x = trow // NY
    y = trow % NY
    a = jnp.where(c == 0, x, y)
    b = jnp.where(c == 0, y, x)
    sa = 4 - 3 * c
    sb = 1 + 3 * c

    def cell(oa, ob):
        return ((a + oa) % 4) * sa + ((b + ob) % 4) * sb

    def remote(src, dst, send_sem, recv_sem, where):
        return pltpu.make_async_remote_copy(
            src_ref=src,
            dst_ref=dst,
            send_sem=send_sem,
            recv_sem=recv_sem,
            device_id=where,
            device_id_type=pl.DeviceIdType.MESH,
        )

    def await_bytes(ref, sem):
        pltpu.make_async_copy(ref, ref, sem).wait()

    sibling = {"rep": other}

    load_r = pltpu.make_async_copy(ratings, rat, lsem.at[0])
    load_u = pltpu.make_async_copy(users.at[pl.ds(HU * c, HU)], u_cur, lsem.at[1])
    load_i = pltpu.make_async_copy(items.at[pl.ds(HI * c, HI)], i_cur, lsem.at[2])
    load_u.start()
    load_i.start()
    load_r.start()

    barrier = pltpu.get_barrier_semaphore()
    for d in range(1, NZ):
        pl.semaphore_signal(
            barrier, inc=1, device_id={"tcol": (z + d) % NZ}, device_id_type=pl.DeviceIdType.MESH
        )
    for d in range(1, NXY):
        pl.semaphore_signal(
            barrier,
            inc=1,
            device_id={"trow": (trow + d) % NXY},
            device_id_type=pl.DeviceIdType.MESH,
        )
    pl.semaphore_signal(barrier, inc=1, device_id=sibling, device_id_type=pl.DeviceIdType.MESH)
    lane = lax.broadcasted_iota(jnp.int32, (TILE, TILE), 1)

    def mask_columns():
        padded = jnp.concatenate(
            [row_mask[...].astype(F32), jnp.zeros((TILE - NT, TILE), F32)], axis=0
        )
        quarter[0, 0] = padded.T

    def make_weights(low, high):
        def one(t, carry):
            spread = jnp.take_along_axis(
                quarter[0, 0], jnp.full((TILE, TILE), t, jnp.int32), axis=1, mode="promise_in_bounds"
            )
            weights[t] = (spread * col_mask[pl.ds(t, 1), :].astype(F32)).astype(BF16)
            return carry

        lax.fori_loop(low, high, one, 0, unroll=4)

    def order_tiles():
        at = lax.broadcasted_iota(jnp.int32, (NT, NT), 0).astype(F32)
        against = lax.broadcasted_iota(jnp.int32, (NT, NT), 1).astype(F32)

        def upright(row):
            return jnp.sum(jnp.where(at == against, row, 0.0), axis=1, keepdims=True)

        def order(row):
            col = upright(row)
            tied = jnp.where(row == col, jnp.where(against < at, 1.0, 0.0), 0.0)
            rank = jnp.sum(jnp.where(row < col, 1.0, tied), axis=1, keepdims=True)
            return col, rank, jnp.where(rank == against, 1.0, 0.0)

        def nearness(slot):
            o = (lax.shift_right_logical(slot, 2) + NZ - z) & (NZ - 1)
            place = jnp.where(o > 4, 2 * (NZ - o) - 1, 2 * o)
            place = jnp.where(o == 4, 7, place)
            return (CAPL * place + (slot & (CAPL - 1))).astype(F32)

        def along(placed, col):
            return jnp.sum(placed * col, axis=0, keepdims=True)

        lanes = lax.broadcasted_iota(jnp.int32, (1, NT), 1)
        row_key, row_rank, row_placed = order(nearness(row_slots[...]))
        col_col, _, col_placed = order(col_slots[...].astype(F32))
        row_col = upright(row_slots[...].astype(F32))
        row_first = jnp.sum(jnp.where(row_key < nearness(lanes), 1.0, 0.0), axis=0, keepdims=True)
        col_first = jnp.sum(jnp.where(col_col < against, 1.0, 0.0), axis=0, keepdims=True)
        table = jnp.concatenate(
            [
                along(row_placed, at[:, 0:1]),
                along(row_placed, row_col),
                along(row_placed, col_col),
                along(col_placed, row_rank),
                along(col_placed, col_col),
                along(col_placed, row_col),
                row_first,
                col_first,
            ],
            axis=0,
        )
        kind = lax.broadcasted_iota(jnp.int32, (8, TILE), 0)
        largest = jnp.where((kind == 0) | (kind == 3) | (kind > 5), NT - 1, NT // 2 - 1)
        table = jnp.concatenate([table, jnp.zeros((8, TILE - NT), F32)], axis=1)
        vtab[...] = jnp.minimum(jnp.maximum(table.astype(jnp.int32), 0), largest)
        pltpu.make_async_copy(vtab, tab, lsem.at[9]).start()

    def make_tables():
        await_bytes(lists_u.at[pl.ds(0, NZ - 1)], lsem.at[3])
        await_bytes(lists_u.at[pl.ds(0, NZ - 1)], lsem.at[4])
        await_bytes(lists_i.at[pl.ds(0, NXY - 1)], lsem.at[5])
        await_bytes(lists_i.at[pl.ds(0, NXY - 1)], lsem.at[6])
        rows_u[...] = jnp.concatenate(
            [lists_u[s, pl.ds(z, 1), :] for s in range(NZ)], axis=0
        )
        rows_i[...] = jnp.concatenate(
            [lists_i[s, pl.ds(trow, 1), :] for s in range(NXY)], axis=0
        )
        down_u = pltpu.make_async_copy(rows_u, slists_u, lsem.at[7])
        down_i = pltpu.make_async_copy(rows_i, slists_i, lsem.at[8])
        down_u.start()
        down_i.start()

    def finish_tables():
        pltpu.make_async_copy(vtab, tab, lsem.at[9]).wait()
        pltpu.make_async_copy(rows_u, slists_u, lsem.at[7]).wait()
        pltpu.make_async_copy(rows_i, slists_i, lsem.at[8]).wait()

        def user_tile(slot):
            source = slot // CAPL
            return source * LT + slists_u[source, slot % CAPL]

        def item_tile(slot):
            source = slot // CAPR
            return source * RT + slists_i[source, slot % CAPR]

        def one(k, carry):
            x_row[k] = user_tile(tab[1, k])
            y_row[k] = item_tile(tab[2, k])
            x_col[k] = user_tile(tab[5, k])
            source = k // LT
            found = jnp.int32(NT)
            for s in range(CAPL):
                found = jnp.where(
                    slists_u[source, s] == k % LT, tab[6, source * CAPL + s], found
                )
            tab_u[k] = found
            source = k // RT
            found = jnp.int32(NT)
            for s in range(CAPR):
                found = jnp.where(
                    slists_i[source, s] == k % RT,
                    tab[7, source * CAPR + s],
                    found,
                )
            tab_i[k] = found
            return carry

        lax.fori_loop(0, NT, one, 0, unroll=2)
        run_u[NT] = jnp.zeros((TILE, TILE), F32)
        run_i[NT] = jnp.zeros((TILE, TILE), F32)

    order_tiles()
    mask_columns()
    make_weights(0, NT)
    load_u.wait()
    load_i.wait()
    pl.semaphore_wait(barrier, NZ - 1 + NXY - 1 + 1)

    names = {}

    def build(it):
        pending = []

        def number(name):
            names.setdefault(name, len(names))
            return names[name]

        def begin(name, src, dst, where):
            n = number(name)
            copy = remote(src, dst, ssem.at[it, n], rsem.at[it, n], where)
            copy.start()
            pending.append(copy)

        def arrive(name, ref):
            await_bytes(ref, rsem.at[it, number(name)])

        def pair_u(o, pr):
            return pool_u.at[it, pl.ds(((z + o) % NZ) * LT + HU * c + 2 * pr, 2)]

        def send_u(way, step, pr):
            ref = pair_u(-way * (step - 1) + NZ, pr)
            begin(("u", way, step, pr), ref, ref, {"tcol": (z + way + NZ) % NZ})

        def sib_u(o, pr):
            ref = pair_u(o, pr)
            n = number(("sg", o % NZ))
            remote(ref, ref, ssem.at[it, n], rsem.at[it, n], sibling).start()

        def other_u(o):
            return pool_u.at[it, pl.ds(((z + o) % NZ) * LT + HU * other, HU)]

        def chunk_i(oa, ob):
            return pool_i.at[it, pl.ds(cell(oa, ob) * RT + HI * c, HI)]

        def tile_i(oa, ob, j):
            return pool_i.at[it, pl.ds(cell(oa, ob) * RT + HI * c + j, 1)]

        def along_a(way):
            return {"trow": cell(way + 4, 0)}

        def along_b(way):
            return {"trow": cell(0, way + 4)}

        def sib_i(oa, ob):
            ref = chunk_i(oa, ob)
            n = number("si")
            remote(ref, ref, ssem.at[it, n], rsem.at[it, n], sibling).start()

        def second_i(oa):
            for way in (1, -1):
                begin(("b", way, oa), chunk_i(oa, 0), chunk_i(oa, 0), along_b(way))

        def start_users():
            for l in range(HU):
                pool_u[it, z * LT + HU * c + l] = u_cur[l].astype(BF16)
            for pr in range(2):
                for way in (1, -1):
                    send_u(way, 1, pr)
            for pr in range(2):
                sib_u(0, pr)

        def start_items():
            for l in range(HI):
                pool_i[it, trow * RT + HI * c + l] = i_cur[l].astype(BF16)
            for way in (1, -1):
                begin(("a", way), chunk_i(0, 0), chunk_i(0, 0), along_a(way))
            second_i(0)
            sib_i(0, 0)

        def gram(ref, count):
            flat = ref[...].reshape(count * TILE, TILE)
            return lax.dot_general(
                flat, flat, (((0,), (0,)), ((), ())), precision=HIGHEST, preferred_element_type=F32
            )

        def start_gram():
            gram_u = gram(u_cur, HU)
            gram_i = gram(i_cur, HI)
            gsend[...] = jnp.where(c == 0, gram_i, gram_u)
            begin("gs", gsend, gsib.at[it], sibling)
            gmine[...] = jnp.where(c == 0, gram_u, gram_i)

        def gram_along_z():
            arrive("gs", gsib.at[it])
            gmine[...] += gsib[it]
            for d in range(1, NZ):
                zz = (z + d) % NZ
                remote(
                    gmine.at[pl.ds(16 * zz, 16)],
                    gz.at[it, d - 1],
                    ssem.at[it, number("gz")],
                    rsem.at[it, number("gz")],
                    {"tcol": zz},
                ).start()

        def gram_across():
            await_bytes(gz.at[it], rsem.at[it, number("gz")])
            total = gmine[pl.ds(16 * z, 16), :]
            for d in range(NZ - 1):
                total = total + gz[it, d]
            gchunk[...] = total
            gxy[it, trow] = total
            for d in range(1, NXY):
                remote(
                    gchunk,
                    gxy.at[it, trow],
                    ssem.at[it, number("gxy")],
                    rsem.at[it, number("gxy")],
                    {"trow": (trow + d) % NXY},
                ).start()

        def gram_whole():
            await_bytes(gxy.at[it, pl.ds(0, NXY - 1)], rsem.at[it, number("gxy")])
            total = gxy[it, 0]
            for d in range(1, NXY):
                total = total + gxy[it, d]
            gsum[...] = total
            gfull[it, pl.ds(16 * z, 16), :] = total
            for d in range(1, NZ):
                remote(
                    gsum,
                    gfull.at[it, pl.ds(16 * z, 16)],
                    ssem.at[it, number("gd")],
                    rsem.at[it, number("gd")],
                    {"tcol": (z + d) % NZ},
                ).start()

        def got_u(way, step, pr):
            arrive(("u", way, step, pr), pair_u(-way * step + NZ, pr))
            if step < 3 or (step == 3 and pr == (0 if way == 1 else 1)):
                send_u(way, step + 1, pr)
            sib_u(-way * step + NZ, pr)

        def first_got(way):
            oa = (4 - way) % 4
            arrive(("a", way), chunk_i(oa, 0))
            j = 0 if way == 1 else 1
            ref = tile_i(oa, 0, j)
            begin(("af", way), ref, ref, along_a(way))
            second_i(oa)
            sib_i(oa, 0)

        def first_far():
            for way, j in ((1, 0), (-1, 1)):
                arrive(("af", way), tile_i(2, 0, j))
            second_i(2)
            sib_i(2, 0)

        def second_got(oa):
            for way, j in ((1, 0), (-1, 1)):
                arrive(("b", way, oa), chunk_i(oa, 4 - way))
                ref = tile_i(oa, 4 - way, j)
                begin(("bf", way, oa), ref, ref, along_b(way))
                sib_i(oa, 4 - way)

        def second_far(oa):
            for way, j in ((1, 0), (-1, 1)):
                arrive(("bf", way, oa), tile_i(oa, 2, j))
            sib_i(oa, 2)

        def at_first(job):
            if it == 0:
                job()

        def error_pass(k, carry):
            t = tab[0, k]
            predicted = lax.dot_general(
                pool_u[it, x_row[k]],
                pool_i[it, y_row[k]],
                (((1,), (1,)), ((), ())),
                preferred_element_type=F32,
            )
            errs[k] = ((predicted - rat[t].astype(F32)) * weights[t].astype(F32)).astype(BF16)
            return carry

        def gather():
            start_gram()
            gram_along_z()
            for pr in range(2):
                for way in (1, -1):
                    got_u(way, 1, pr)
            first_got(1)
            first_got(-1)
            second_got(0)
            at_first(make_tables)
            first_far()
            for pr in range(2):
                for way in (1, -1):
                    got_u(way, 2, pr)
            second_got(3)
            second_got(1)
            second_far(0)
            for way in (1, -1):
                got_u(way, 3, 0)
            gram_across()
            second_got(2)
            for way in (1, -1):
                got_u(way, 3, 1)
            second_far(3)
            second_far(1)
            second_far(2)
            at_first(finish_tables)
            at_first(load_r.wait)
            arrive("si", pool_i.at[it, pl.ds(0, NT // 2)])
            got_u(1, 4, 0)
            got_u(-1, 4, 1)
            for o in range(NZ):
                arrive(("sg", o), other_u(o))
            lax.fori_loop(0, NT, error_pass, 0, unroll=8)

        zero = jnp.zeros((TILE, TILE), F32)

        def item_pass(n, carry):
            k = NT - 1 - n
            run, before = carry
            slot = tab[4, k]
            term = lax.dot_general(
                errs[tab[3, k]],
                pool_u[it, x_col[k]],
                (((0,), (0,)), ((), ())),
                preferred_element_type=F32,
            )
            run = jnp.where(slot == before, run, 0.0) + term
            run_i[k] = run
            return run, slot

        def share_i(ob):
            def one(oa, carry, ob=ob):
                p = ((b + oa) % 4) * sb + ((a + ob) % 4) * sa
                q = p * RT + HI * other
                for j in range(HI):
                    sibs_i[ob, oa, j] = run_i[tab_i[q + j]].astype(BF16)
                return carry

            lax.fori_loop(0, 4, one, 0)
            begin(("shi", ob), sibs_i.at[ob], sibr_i.at[it, ob], sibling)

        def user_pass(n, carry):
            k = NT - 1 - n
            run, before = carry
            slot = tab[1, k]
            term = jnp.dot(errs[k], pool_i[it, y_row[k]], preferred_element_type=F32)
            run = jnp.where(slot == before, run, 0.0) + term
            run_u[k] = run
            return run, slot

        def terms():
            lax.fori_loop(0, NT, item_pass, (zero, jnp.int32(-1)), unroll=8)
            for ob in (2, 1, 3, 0):
                share_i(ob)
            carry = lax.fori_loop(0, 36, user_pass, (zero, jnp.int32(-1)), unroll=6)
            share_u(4)
            for n, o in enumerate((3, 5, 2, 6, 1, 7, 0)):
                carry = lax.fori_loop(36 + 4 * n, 40 + 4 * n, user_pass, carry, unroll=4)
                share_u(o)

        def own_u(o, l):
            p = ((z + o) % NZ) * LT + HU * c + l
            return run_u[tab_u[p]]

        def share_u(o):
            def one(l, carry):
                p = ((z + o) % NZ) * LT + HU * other + l
                sibs_u[o, l] = run_u[tab_u[p]].astype(BF16)
                return carry

            lax.fori_loop(0, HU, one, 0)
            begin(("su", o), sibs_u.at[o], sibr_u.at[it, o], sibling)

        def ring_send(w, k, pr):
            ref = ring_s.at[w, k, pl.ds(2 * pr, 2)]
            begin(
                ("r", w, k, pr),
                ref,
                ring_r.at[it, w, k, pl.ds(2 * pr, 2)],
                {"tcol": (z + (1, NZ - 1)[w]) % NZ},
            )

        def ring_first(w):
            for l in (2 * w, 2 * w + 1):
                ring_s[w, 0, l] = (own_u(4, l) + sibr_u[it, 4, l].astype(F32)).astype(BF16)
            ring_send(w, 0, w)

        def ring_pair(w, k, pr, held):
            o = (4 - k) if w == 0 else 4 + k
            if held:
                arrive(("r", w, k - 1, pr), ring_r.at[it, w, k - 1, pl.ds(2 * pr, 2)])
            for l in (2 * pr, 2 * pr + 1):
                value = own_u(o, l) + sibr_u[it, o, l].astype(F32)
                if held:
                    value = value + ring_r[it, w, k - 1, l].astype(F32)
                ring_s[w, k, l] = value.astype(BF16)
            ring_send(w, k, pr)

        def ring_second(w):
            o = (3, 5)[w]
            arrive(("su", o), sibr_u.at[it, o])
            ring_pair(w, 1, 1 - w, False)

        def ring_step(w, k):
            o = (4 - k) if w == 0 else 4 + k
            if k > 1:
                arrive(("su", o), sibr_u.at[it, o])
                ring_pair(w, k, 1 - w, True)
            ring_pair(w, k, w, True)

        def own_i(oa, ob, j):
            p = cell(oa, ob)
            q = p * RT + HI * c + j
            return run_i[tab_i[q]] + sibr_i[it, ob, oa, j].astype(F32)

        def half_b():
            arrive(("shi", 2), sibr_i.at[it, 2])
            for w, ob in ((0, 1), (1, 3)):

                def one(o, carry, w=w):
                    half_s[w, o] = own_i(o, 2, w).astype(BF16)
                    return carry

                lax.fori_loop(0, 4, one, 0)
                begin(("h", w), half_s.at[w], half_r.at[it, w], {"trow": cell(0, ob)})

        def eliminate(k, carry):
            mat = gfull[it]
            row = gfull[it, pl.ds(k, 1), :]
            pick = jnp.full((TILE, TILE), k, jnp.int32)
            column = jnp.take_along_axis(mat, pick, axis=1, mode="promise_in_bounds")
            pivot = jnp.sum(jnp.where(lane[0:1] == k, row, 0.0), axis=1, keepdims=True)
            scaled = jnp.where(lane[0:1] == k, 1.0, row) / pivot
            gfull[it] = jnp.where(lane == k, 0.0, mat) - column * scaled
            gfull[it, pl.ds(k, 1), :] = scaled
            return carry

        def invert(low, high):
            lax.fori_loop(low, high, eliminate, 0)

        def fold_b(w, ob):
            arrive(("h", w), half_r.at[it, w])
            arrive(("shi", ob), sibr_i.at[it, ob])

            def one(o, carry):
                for j in range(HI):
                    value = own_i(o, ob, j)
                    if j == w:
                        value = value + half_r[it, w, o].astype(F32)
                    full_s[w, o, j] = value.astype(BF16)
                return carry

            lax.fori_loop(0, 4, one, 0)
            for o in (2, 1, 3, 0):
                begin(
                    ("f", w, o), full_s.at[w, o], full_r.at[it, w, o], {"trow": cell(0, ob)}
                )

        def take_b(o):
            for w in range(2):
                arrive(("f", w, o), full_r.at[it, w, o])
            for j in range(HI):
                quarter[o, j] = (
                    own_i(o, 0, j) + full_r[it, 0, o, j].astype(F32) + full_r[it, 1, o, j].astype(F32)
                )

        def half_a():
            for w, oa in ((0, 1), (1, 3)):
                ah_s[w] = quarter[2, w].astype(BF16)
                begin(("ah", w), ah_s.at[w], ah_r.at[it, w], {"trow": cell(oa, 0)})

        def fold_a():
            for w, oa in ((0, 1), (1, 3)):
                arrive(("ah", w), ah_r.at[it, w])
                for j in range(HI):
                    value = quarter[oa, j]
                    if j == w:
                        value = value + ah_r[it, w].astype(F32)
                    af_s[w, j] = value.astype(BF16)
                begin(("af2", w), af_s.at[w], af_r.at[it, w], {"trow": cell(oa, 0)})

        def reduce(after_users, after_items):
            half_b()
            arrive(("su", 4), sibr_u.at[it, 4])
            ring_first(0)
            ring_first(1)
            ring_second(0)
            ring_second(1)
            await_bytes(gfull.at[it, pl.ds(0, 16 * (NZ - 1))], rsem.at[it, number("gd")])
            invert(0, 8)
            ring_step(0, 1)
            ring_step(1, 1)
            fold_b(0, 1)
            fold_b(1, 3)
            invert(8, 24)
            ring_step(0, 2)
            ring_step(1, 2)
            arrive(("shi", 0), sibr_i.at[it, 0])
            take_b(2)
            half_a()
            take_b(1)
            take_b(3)
            invert(24, 40)
            ring_step(0, 3)
            ring_step(1, 3)
            fold_a()
            take_b(0)
            invert(40, TILE)
            finish(after_users, after_items)

        def finish(after_users, after_items):
            begin("inv", gfull.at[it], gother.at[it], sibling)
            arrive(("su", 0), sibr_u.at[it, 0])
            for w in range(2):
                for pr in range(2):
                    arrive(("r", w, 3, pr), ring_r.at[it, w, 3, pl.ds(2 * pr, 2)])
            grad_u = jnp.concatenate(
                [
                    own_u(0, l)
                    + sibr_u[it, 0, l].astype(F32)
                    + ring_r[it, 0, 3, l].astype(F32)
                    + ring_r[it, 1, 3, l].astype(F32)
                    for l in range(HU)
                ],
                axis=0,
            )
            arrive("inv", gother.at[it])
            inverse_i = jnp.where(c == 0, gother[it], gfull[it])
            step_u = jnp.dot(grad_u, inverse_i, precision=HIGHEST, preferred_element_type=F32)
            u_cur[...] = u_cur[...] - user_coef * step_u.reshape(HU, TILE, TILE)
            after_users()
            for w in range(2):
                arrive(("af2", w), af_r.at[it, w])
            grad_i = jnp.concatenate(
                [
                    quarter[0, j] + af_r[it, 0, j].astype(F32) + af_r[it, 1, j].astype(F32)
                    for j in range(HI)
                ],
                axis=0,
            )
            inverse_u = jnp.where(c == 0, gfull[it], gother[it])
            step_i = jnp.dot(grad_i, inverse_u, precision=HIGHEST, preferred_element_type=F32)
            i_cur[...] = i_cur[...] - item_coef * step_i.reshape(HI, TILE, TILE)
            after_items()

        def drain():
            for copy in pending:
                copy.wait_send()
            for o in range(NZ):
                await_bytes(other_u(o), ssem.at[it, number(("sg", o))])
            await_bytes(pool_i.at[it, pl.ds(0, NT // 2)], ssem.at[it, number("si")])
            await_bytes(gz.at[it], ssem.at[it, number("gz")])
            await_bytes(gxy.at[it, pl.ds(0, NXY - 1)], ssem.at[it, number("gxy")])
            await_bytes(gfull.at[it, pl.ds(0, 16 * (NZ - 1))], ssem.at[it, number("gd")])
            assert len(names) <= 128, len(names)

        return start_users, start_items, gather, gram_whole, terms, reduce, drain

    def send_lists():
        for d in range(1, NZ):
            remote(
                sends.at[pl.ds(0, NZ)], lists_u.at[z], lsem.at[3], lsem.at[4], {"tcol": (z + d) % NZ}
            ).start()
        for d in range(1, NXY):
            remote(
                sends.at[pl.ds(NZ, NXY)],
                lists_i.at[trow],
                lsem.at[5],
                lsem.at[6],
                {"trow": (trow + d) % NXY},
            ).start()
        lists_u[z] = sends[0:NZ, :]
        lists_i[trow] = sends[NZ : NZ + NXY, :]

    last_u = remote(u_cur, out_u.at[pl.ds(HU * c, HU)], lsem.at[1], lsem.at[7], sibling)
    last_i = remote(i_cur, out_i.at[pl.ds(HI * c, HI)], lsem.at[2], lsem.at[8], sibling)
    phases = [build(it) for it in range(ITERS)]
    phases[0][0]()
    phases[0][1]()
    send_lists()
    for it in range(ITERS):
        _, _, gather, gram_whole, terms, reduce, drain = phases[it]
        gather()
        gram_whole()
        terms()
        if it + 1 < ITERS:
            reduce(phases[it + 1][0], phases[it + 1][1])
        else:
            reduce(last_u.start, last_i.start)
        drain()

    for l in range(HU):
        out_u[HU * c + l] = u_cur[l]
    for l in range(HI):
        out_i[HI * c + l] = i_cur[l]
    last_u.wait()
    last_i.wait()


def write_out(new_u, new_i, out_u, out_i, sems):
    put_u = pltpu.make_async_copy(new_u, out_u, sems.at[0])
    put_i = pltpu.make_async_copy(new_i, out_i, sems.at[1])
    put_u.start()
    put_i.start()
    put_u.wait()
    put_i.wait()


def on_device(
    users, items, ratings, row_mask, col_mask, row_slots, col_slots, send_users, send_items
):
    own_users = users.shape[0] // TILE
    own_items = items.shape[0] // TILE
    all_users = own_users * TILE * NXY * NZ
    all_items = own_items * TILE * NXY * NZ
    user_coef = 2.0 * all_items * own_users / (TILE * NT * 2)
    item_coef = 2.0 * all_users * own_items / (TILE * NT * 2)
    sends = jnp.concatenate(
        [
            jnp.pad(send_users.reshape(NZ, CAPL), ((0, 0), (0, TILE - CAPL))),
            jnp.pad(send_items.reshape(NXY, CAPR), ((0, 0), (0, TILE - CAPR))),
        ],
        axis=0,
    )

    any_spec = pl.BlockSpec(memory_space=pl.ANY)
    vmem_spec = pl.BlockSpec(memory_space=pltpu.VMEM)
    square = (TILE, TILE)
    table = pltpu.SMEM((NT,), jnp.int32)
    out_u, out_i = pl.pallas_call(
        functools.partial(kernel, user_coef, item_coef),
        out_shape=(
            jax.ShapeDtypeStruct((LT,) + square, F32),
            jax.ShapeDtypeStruct((RT,) + square, F32),
        ),
        in_specs=[vmem_spec] * 5 + [any_spec] * 3,
        out_specs=(vmem_spec, vmem_spec),
        scratch_shapes=[
            pltpu.VMEM((NZ, NZ, TILE), jnp.int32),
            pltpu.VMEM((NXY, NXY, TILE), jnp.int32),
            pltpu.VMEM((NZ, TILE), jnp.int32),
            pltpu.VMEM((NXY, TILE), jnp.int32),
            pltpu.SMEM((NZ, TILE), jnp.int32),
            pltpu.SMEM((NXY, TILE), jnp.int32),
            pltpu.VMEM((8, TILE), jnp.int32),
            pltpu.SMEM((8, TILE), jnp.int32),
            table,
            table,
            table,
            table,
            table,
            pltpu.VMEM((HU,) + square, F32),
            pltpu.VMEM((HI,) + square, F32),
            pltpu.VMEM((NT,) + square, BF16),
            pltpu.VMEM((NT,) + square, BF16),
            pltpu.VMEM((ITERS, NT) + square, BF16),
            pltpu.VMEM((ITERS, NT) + square, BF16),
            pltpu.VMEM((NT,) + square, BF16),
            pltpu.VMEM((NT + 1,) + square, F32),
            pltpu.VMEM((NT + 1,) + square, F32),
            pltpu.VMEM(square, F32),
            pltpu.VMEM(square, F32),
            pltpu.VMEM((ITERS,) + square, F32),
            pltpu.VMEM((ITERS, NZ - 1, 16, TILE), F32),
            pltpu.VMEM((16, TILE), F32),
            pltpu.VMEM((ITERS, NXY, 16, TILE), F32),
            pltpu.VMEM((16, TILE), F32),
            pltpu.VMEM((ITERS,) + square, F32),
            pltpu.VMEM((ITERS,) + square, F32),
            pltpu.VMEM((NZ, HU) + square, BF16),
            pltpu.VMEM((ITERS, NZ, HU) + square, BF16),
            pltpu.VMEM((2, 4, HU) + square, BF16),
            pltpu.VMEM((ITERS, 2, 4, HU) + square, BF16),
            pltpu.VMEM((4, 4, HI) + square, BF16),
            pltpu.VMEM((ITERS, 4, 4, HI) + square, BF16),
            pltpu.VMEM((2, 4) + square, BF16),
            pltpu.VMEM((ITERS, 2, 4) + square, BF16),
            pltpu.VMEM((2, 4, HI) + square, BF16),
            pltpu.VMEM((ITERS, 2, 4, HI) + square, BF16),
            pltpu.VMEM((4, HI) + square, F32),
            pltpu.VMEM((2,) + square, BF16),
            pltpu.VMEM((ITERS, 2) + square, BF16),
            pltpu.VMEM((2, HI) + square, BF16),
            pltpu.VMEM((ITERS, 2, HI) + square, BF16),
            pltpu.SemaphoreType.DMA((ITERS, 128)),
            pltpu.SemaphoreType.DMA((ITERS, 128)),
            pltpu.SemaphoreType.DMA((10,)),
        ],
        compiler_params=pltpu.CompilerParams(
            collective_id=0, has_side_effects=True, vmem_limit_bytes=60 * 1024 * 1024
        ),
        name="scaled_gd",
    )(
        row_slots.reshape(1, NT),
        col_slots.reshape(1, NT),
        sends,
        row_mask.reshape(NT, TILE),
        col_mask.reshape(NT, TILE),
        users.reshape((LT,) + square),
        items.reshape((RT,) + square),
        ratings.reshape((NT,) + square),
    )
    out_u, out_i = pl.pallas_call(
        write_out,
        out_shape=(
            jax.ShapeDtypeStruct((LT,) + square, F32),
            jax.ShapeDtypeStruct((RT,) + square, F32),
        ),
        in_specs=[vmem_spec, vmem_spec],
        out_specs=(any_spec, any_spec),
        scratch_shapes=[pltpu.SemaphoreType.DMA((2,))],
        name="write_out",
    )(out_u, out_i)
    return out_u.reshape(users.shape), out_i.reshape(items.shape)


def solution(mesh):
    return jax.shard_map(
        on_device,
        mesh=mesh,
        in_specs=(
            P(("trow", "tcol"), None),
            P(("tcol", "trow"), None),
            P("trow", "tcol", "rep", None, None, None),
            P("trow", "tcol", "rep", None, None),
            P("trow", "tcol", "rep", None, None),
            P("trow", "tcol", "rep", None),
            P("trow", "tcol", "rep", None),
            P("trow", "tcol", "rep", None, None),
            P("trow", "tcol", "rep", None, None),
        ),
        out_specs=(P(("trow", "tcol"), None), P(("tcol", "trow"), None)),
        check_vma=False,
    )
```

```python
import functools

import jax
import jax.numpy as jnp
from jax import lax
from jax.experimental import pallas as pl
from jax.experimental.pallas import tpu as pltpu
from jax.sharding import PartitionSpec as P

ITERS = 2
TILE = 128
NX = 4
NY = 4
NZ = 8
NXY = NX * NY
LT = 8
RT = 4
NT = 64
CAPL = 4
CAPR = 2
HU = LT // 2
HI = RT // 2
F32 = jnp.float32
BF16 = jnp.bfloat16
HIGHEST = lax.Precision.HIGHEST


def kernel(
    user_coef,
    item_coef,
    row_slots,
    col_slots,
    sends,
    row_mask,
    col_mask,
    users,
    items,
    ratings,
    out_u,
    out_i,
    lists_u,
    lists_i,
    rows_u,
    rows_i,
    slists_u,
    slists_i,
    vtab,
    tab,
    x_row,
    y_row,
    x_col,
    tab_u,
    tab_i,
    u_cur,
    i_cur,
    rat,
    weights,
    pool_u,
    pool_i,
    errs,
    run_u,
    run_i,
    gmine,
    gsend,
    gsib,
    gz,
    gchunk,
    gxy,
    gsum,
    gfull,
    gother,
    sibs_u,
    sibr_u,
    ring_s,
    ring_r,
    sibs_i,
    sibr_i,
    half_s,
    half_r,
    full_s,
    full_r,
    quarter,
    ah_s,
    ah_r,
    af_s,
    af_r,
    ssem,
    rsem,
    lsem,
):
    trow = lax.axis_index("trow")
    z = lax.axis_index("tcol")
    c = lax.axis_index("rep")
    other = 1 - c
    x = trow // NY
    y = trow % NY
    a = jnp.where(c == 0, x, y)
    b = jnp.where(c == 0, y, x)
    sa = 4 - 3 * c
    sb = 1 + 3 * c

    def cell(oa, ob):
        return ((a + oa) % 4) * sa + ((b + ob) % 4) * sb

    def remote(src, dst, send_sem, recv_sem, where):
        return pltpu.make_async_remote_copy(
            src_ref=src,
            dst_ref=dst,
            send_sem=send_sem,
            recv_sem=recv_sem,
            device_id=where,
            device_id_type=pl.DeviceIdType.MESH,
        )

    def await_bytes(ref, sem):
        pltpu.make_async_copy(ref, ref, sem).wait()

    sibling = {"rep": other}

    load_r = pltpu.make_async_copy(ratings, rat, lsem.at[0])
    load_u = pltpu.make_async_copy(users.at[pl.ds(HU * c, HU)], u_cur, lsem.at[1])
    load_i = pltpu.make_async_copy(items.at[pl.ds(HI * c, HI)], i_cur, lsem.at[2])
    load_u.start()
    load_i.start()
    load_r.start()

    barrier = pltpu.get_barrier_semaphore()
    for d in range(1, NZ):
        pl.semaphore_signal(
            barrier, inc=1, device_id={"tcol": (z + d) % NZ}, device_id_type=pl.DeviceIdType.MESH
        )
    for d in range(1, NXY):
        pl.semaphore_signal(
            barrier,
            inc=1,
            device_id={"trow": (trow + d) % NXY},
            device_id_type=pl.DeviceIdType.MESH,
        )
    pl.semaphore_signal(barrier, inc=1, device_id=sibling, device_id_type=pl.DeviceIdType.MESH)
    lane8 = lax.broadcasted_iota(jnp.int32, (8, TILE), 1)

    def mask_columns():
        padded = jnp.concatenate(
            [row_mask[...].astype(F32), jnp.zeros((TILE - NT, TILE), F32)], axis=0
        )
        quarter[0, 0] = padded.T

    def make_weights(low, high):
        def one(t, carry):
            spread = jnp.take_along_axis(
                quarter[0, 0], jnp.full((TILE, TILE), t, jnp.int32), axis=1, mode="promise_in_bounds"
            )
            weights[t] = (spread * col_mask[pl.ds(t, 1), :].astype(F32)).astype(BF16)
            return carry

        lax.fori_loop(low, high, one, 0, unroll=4)

    def order_tiles():
        at = lax.broadcasted_iota(jnp.int32, (NT, NT), 0).astype(F32)
        against = lax.broadcasted_iota(jnp.int32, (NT, NT), 1).astype(F32)

        def upright(row):
            return jnp.sum(jnp.where(at == against, row, 0.0), axis=1, keepdims=True)

        def order(row):
            col = upright(row)
            tied = jnp.where(row == col, jnp.where(against < at, 1.0, 0.0), 0.0)
            rank = jnp.sum(jnp.where(row < col, 1.0, tied), axis=1, keepdims=True)
            return col, rank, jnp.where(rank == against, 1.0, 0.0)

        def nearness(slot):
            o = (lax.shift_right_logical(slot, 2) + NZ - z) & (NZ - 1)
            place = jnp.where(o > 4, 2 * (NZ - o) - 1, 2 * o)
            place = jnp.where(o == 4, 7, place)
            return (CAPL * place + (slot & (CAPL - 1))).astype(F32)

        def along(placed, col):
            return jnp.sum(placed * col, axis=0, keepdims=True)

        lanes = lax.broadcasted_iota(jnp.int32, (1, NT), 1)
        row_key, row_rank, row_placed = order(nearness(row_slots[...]))
        col_col, _, col_placed = order(col_slots[...].astype(F32))
        row_col = upright(row_slots[...].astype(F32))
        row_first = jnp.sum(jnp.where(row_key < nearness(lanes), 1.0, 0.0), axis=0, keepdims=True)
        col_first = jnp.sum(jnp.where(col_col < against, 1.0, 0.0), axis=0, keepdims=True)
        table = jnp.concatenate(
            [
                along(row_placed, at[:, 0:1]),
                along(row_placed, row_col),
                along(row_placed, col_col),
                along(col_placed, row_rank),
                along(col_placed, col_col),
                along(col_placed, row_col),
                row_first,
                col_first,
            ],
            axis=0,
        )
        kind = lax.broadcasted_iota(jnp.int32, (8, TILE), 0)
        largest = jnp.where((kind == 0) | (kind == 3) | (kind > 5), NT - 1, NT // 2 - 1)
        table = jnp.concatenate([table, jnp.zeros((8, TILE - NT), F32)], axis=1)
        vtab[...] = jnp.minimum(jnp.maximum(table.astype(jnp.int32), 0), largest)
        pltpu.make_async_copy(vtab, tab, lsem.at[9]).start()

    def make_tables():
        await_bytes(lists_u.at[pl.ds(0, NZ - 1)], lsem.at[3])
        await_bytes(lists_u.at[pl.ds(0, NZ - 1)], lsem.at[4])
        await_bytes(lists_i.at[pl.ds(0, NXY - 1)], lsem.at[5])
        await_bytes(lists_i.at[pl.ds(0, NXY - 1)], lsem.at[6])
        rows_u[...] = jnp.concatenate(
            [lists_u[s, pl.ds(z, 1), :] for s in range(NZ)], axis=0
        )
        rows_i[...] = jnp.concatenate(
            [lists_i[s, pl.ds(trow, 1), :] for s in range(NXY)], axis=0
        )
        down_u = pltpu.make_async_copy(rows_u, slists_u, lsem.at[7])
        down_i = pltpu.make_async_copy(rows_i, slists_i, lsem.at[8])
        down_u.start()
        down_i.start()

    def finish_tables():
        pltpu.make_async_copy(vtab, tab, lsem.at[9]).wait()
        pltpu.make_async_copy(rows_u, slists_u, lsem.at[7]).wait()
        pltpu.make_async_copy(rows_i, slists_i, lsem.at[8]).wait()

        def user_tile(slot):
            source = slot // CAPL
            return source * LT + slists_u[source, slot % CAPL]

        def item_tile(slot):
            source = slot // CAPR
            return source * RT + slists_i[source, slot % CAPR]

        def one(k, carry):
            x_row[k] = user_tile(tab[1, k])
            y_row[k] = item_tile(tab[2, k])
            x_col[k] = user_tile(tab[5, k])
            source = k // LT
            found = jnp.int32(NT)
            for s in range(CAPL):
                found = jnp.where(
                    slists_u[source, s] == k % LT, tab[6, source * CAPL + s], found
                )
            tab_u[k] = found
            source = k // RT
            found = jnp.int32(NT)
            for s in range(CAPR):
                found = jnp.where(
                    slists_i[source, s] == k % RT,
                    tab[7, source * CAPR + s],
                    found,
                )
            tab_i[k] = found
            return carry

        lax.fori_loop(0, NT, one, 0, unroll=2)
        run_u[NT] = jnp.zeros((TILE, TILE), F32)
        run_i[NT] = jnp.zeros((TILE, TILE), F32)

    order_tiles()
    mask_columns()
    make_weights(0, NT)
    load_u.wait()
    load_i.wait()
    pl.semaphore_wait(barrier, NZ - 1 + NXY - 1 + 1)

    names = {}

    def build(it):
        pending = []

        def number(name):
            names.setdefault(name, len(names))
            return names[name]

        def begin(name, src, dst, where):
            n = number(name)
            copy = remote(src, dst, ssem.at[it, n], rsem.at[it, n], where)
            copy.start()
            pending.append(copy)

        def arrive(name, ref):
            await_bytes(ref, rsem.at[it, number(name)])

        def pair_u(o, pr):
            return pool_u.at[it, pl.ds(((z + o) % NZ) * LT + HU * c + 2 * pr, 2)]

        def send_u(way, step, pr):
            ref = pair_u(-way * (step - 1) + NZ, pr)
            begin(("u", way, step, pr), ref, ref, {"tcol": (z + way + NZ) % NZ})

        def sib_u(o, pr):
            ref = pair_u(o, pr)
            n = number(("sg", o % NZ))
            remote(ref, ref, ssem.at[it, n], rsem.at[it, n], sibling).start()

        def other_u(o):
            return pool_u.at[it, pl.ds(((z + o) % NZ) * LT + HU * other, HU)]

        def chunk_i(oa, ob):
            return pool_i.at[it, pl.ds(cell(oa, ob) * RT + HI * c, HI)]

        def tile_i(oa, ob, j):
            return pool_i.at[it, pl.ds(cell(oa, ob) * RT + HI * c + j, 1)]

        def along_a(way):
            return {"trow": cell(way + 4, 0)}

        def along_b(way):
            return {"trow": cell(0, way + 4)}

        def sib_i(oa, ob):
            ref = chunk_i(oa, ob)
            n = number("si")
            remote(ref, ref, ssem.at[it, n], rsem.at[it, n], sibling).start()

        def second_i(oa):
            for way in (1, -1):
                begin(("b", way, oa), chunk_i(oa, 0), chunk_i(oa, 0), along_b(way))

        def start_users():
            for l in range(HU):
                pool_u[it, z * LT + HU * c + l] = u_cur[l].astype(BF16)
            for pr in range(2):
                for way in (1, -1):
                    send_u(way, 1, pr)
            for pr in range(2):
                sib_u(0, pr)

        def start_items():
            for l in range(HI):
                pool_i[it, trow * RT + HI * c + l] = i_cur[l].astype(BF16)
            for way in (1, -1):
                begin(("a", way), chunk_i(0, 0), chunk_i(0, 0), along_a(way))
            second_i(0)
            sib_i(0, 0)

        def gram(ref, count):
            flat = ref[...].reshape(count * TILE, TILE)
            return lax.dot_general(
                flat, flat, (((0,), (0,)), ((), ())), precision=HIGHEST, preferred_element_type=F32
            )

        def start_gram():
            gram_u = gram(u_cur, HU)
            gram_i = gram(i_cur, HI)
            gsend[...] = jnp.where(c == 0, gram_i, gram_u)
            begin("gs", gsend, gsib.at[it], sibling)
            gmine[...] = jnp.where(c == 0, gram_u, gram_i)

        def gram_along_z():
            arrive("gs", gsib.at[it])
            gmine[...] += gsib[it]
            for d in range(1, NZ):
                zz = (z + d) % NZ
                remote(
                    gmine.at[pl.ds(16 * zz, 16)],
                    gz.at[it, d - 1],
                    ssem.at[it, number("gz")],
                    rsem.at[it, number("gz")],
                    {"tcol": zz},
                ).start()

        def gram_across():
            await_bytes(gz.at[it], rsem.at[it, number("gz")])
            total = gmine[pl.ds(16 * z, 16), :]
            for d in range(NZ - 1):
                total = total + gz[it, d]
            gchunk[...] = total
            gxy[it, trow] = total
            for d in range(1, NXY):
                remote(
                    gchunk,
                    gxy.at[it, trow],
                    ssem.at[it, number("gxy")],
                    rsem.at[it, number("gxy")],
                    {"trow": (trow + d) % NXY},
                ).start()

        def gram_whole():
            await_bytes(gxy.at[it, pl.ds(0, NXY - 1)], rsem.at[it, number("gxy")])
            total = gxy[it, 0]
            for d in range(1, NXY):
                total = total + gxy[it, d]
            gsum[...] = total
            gfull[it, pl.ds(16 * z, 16), :] = total
            for d in range(1, NZ):
                remote(
                    gsum,
                    gfull.at[it, pl.ds(16 * z, 16)],
                    ssem.at[it, number("gd")],
                    rsem.at[it, number("gd")],
                    {"tcol": (z + d) % NZ},
                ).start()

        def got_u(way, step, pr):
            arrive(("u", way, step, pr), pair_u(-way * step + NZ, pr))
            if step < 3 or (step == 3 and pr == (0 if way == 1 else 1)):
                send_u(way, step + 1, pr)
            sib_u(-way * step + NZ, pr)

        def first_got(way):
            oa = (4 - way) % 4
            arrive(("a", way), chunk_i(oa, 0))
            j = 0 if way == 1 else 1
            ref = tile_i(oa, 0, j)
            begin(("af", way), ref, ref, along_a(way))
            second_i(oa)
            sib_i(oa, 0)

        def first_far():
            for way, j in ((1, 0), (-1, 1)):
                arrive(("af", way), tile_i(2, 0, j))
            second_i(2)
            sib_i(2, 0)

        def second_got(oa):
            for way, j in ((1, 0), (-1, 1)):
                arrive(("b", way, oa), chunk_i(oa, 4 - way))
                ref = tile_i(oa, 4 - way, j)
                begin(("bf", way, oa), ref, ref, along_b(way))
                sib_i(oa, 4 - way)

        def second_far(oa):
            for way, j in ((1, 0), (-1, 1)):
                arrive(("bf", way, oa), tile_i(oa, 2, j))
            sib_i(oa, 2)

        def at_first(job):
            if it == 0:
                job()

        def error_pass(k, carry):
            t = tab[0, k]
            predicted = lax.dot_general(
                pool_u[it, x_row[k]],
                pool_i[it, y_row[k]],
                (((1,), (1,)), ((), ())),
                preferred_element_type=F32,
            )
            errs[k] = ((predicted - rat[t].astype(F32)) * weights[t].astype(F32)).astype(BF16)
            return carry

        def gather():
            start_gram()
            gram_along_z()
            for pr in range(2):
                for way in (1, -1):
                    got_u(way, 1, pr)
            first_got(1)
            first_got(-1)
            second_got(0)
            at_first(make_tables)
            first_far()
            for pr in range(2):
                for way in (1, -1):
                    got_u(way, 2, pr)
            second_got(3)
            second_got(1)
            second_far(0)
            for way in (1, -1):
                got_u(way, 3, 0)
            gram_across()
            second_got(2)
            for way in (1, -1):
                got_u(way, 3, 1)
            second_far(3)
            second_far(1)
            second_far(2)
            at_first(finish_tables)
            at_first(load_r.wait)
            arrive("si", pool_i.at[it, pl.ds(0, NT // 2)])
            got_u(1, 4, 0)
            got_u(-1, 4, 1)
            for o in range(NZ):
                arrive(("sg", o), other_u(o))
            lax.fori_loop(0, 16, error_pass, 0, unroll=8)
            gram_whole()
            lax.fori_loop(16, NT, error_pass, 0, unroll=8)

        zero = jnp.zeros((TILE, TILE), F32)

        def item_pass(n, carry):
            k = NT - 1 - n
            run, before = carry
            slot = tab[4, k]
            term = lax.dot_general(
                errs[tab[3, k]],
                pool_u[it, x_col[k]],
                (((0,), (0,)), ((), ())),
                preferred_element_type=F32,
            )
            run = jnp.where(slot == before, run, 0.0) + term
            run_i[k] = run
            return run, slot

        def share_i(ob):
            def one(oa, carry, ob=ob):
                p = ((b + oa) % 4) * sb + ((a + ob) % 4) * sa
                q = p * RT + HI * other
                for j in range(HI):
                    sibs_i[ob, oa, j] = run_i[tab_i[q + j]].astype(BF16)
                return carry

            lax.fori_loop(0, 4, one, 0)
            begin(("shi", ob), sibs_i.at[ob], sibr_i.at[it, ob], sibling)

        def user_pass(n, carry):
            k = NT - 1 - n
            run, before = carry
            slot = tab[1, k]
            term = jnp.dot(errs[k], pool_i[it, y_row[k]], preferred_element_type=F32)
            run = jnp.where(slot == before, run, 0.0) + term
            run_u[k] = run
            return run, slot

        def terms():
            lax.fori_loop(0, NT, item_pass, (zero, jnp.int32(-1)), unroll=8)
            for ob in (2, 1, 3, 0):
                share_i(ob)
            carry = lax.fori_loop(0, 36, user_pass, (zero, jnp.int32(-1)), unroll=9)
            share_u(4)
            for n, o in enumerate((3, 5, 2, 6, 1, 7, 0)):
                carry = lax.fori_loop(36 + 4 * n, 40 + 4 * n, user_pass, carry, unroll=4)
                share_u(o)

        def own_u(o, l):
            p = ((z + o) % NZ) * LT + HU * c + l
            return run_u[tab_u[p]]

        def share_u(o):
            def one(l, carry):
                p = ((z + o) % NZ) * LT + HU * other + l
                sibs_u[o, l] = run_u[tab_u[p]].astype(BF16)
                return carry

            lax.fori_loop(0, HU, one, 0)
            begin(("su", o), sibs_u.at[o], sibr_u.at[it, o], sibling)

        def ring_send(w, k, pr):
            ref = ring_s.at[w, k, pl.ds(2 * pr, 2)]
            begin(
                ("r", w, k, pr),
                ref,
                ring_r.at[it, w, k, pl.ds(2 * pr, 2)],
                {"tcol": (z + (1, NZ - 1)[w]) % NZ},
            )

        def ring_first(w):
            for l in (2 * w, 2 * w + 1):
                ring_s[w, 0, l] = (own_u(4, l) + sibr_u[it, 4, l].astype(F32)).astype(BF16)
            ring_send(w, 0, w)

        def ring_pair(w, k, pr, held):
            o = (4 - k) if w == 0 else 4 + k
            if held:
                arrive(("r", w, k - 1, pr), ring_r.at[it, w, k - 1, pl.ds(2 * pr, 2)])
            for l in (2 * pr, 2 * pr + 1):
                value = own_u(o, l) + sibr_u[it, o, l].astype(F32)
                if held:
                    value = value + ring_r[it, w, k - 1, l].astype(F32)
                ring_s[w, k, l] = value.astype(BF16)
            ring_send(w, k, pr)

        def ring_second(w):
            o = (3, 5)[w]
            arrive(("su", o), sibr_u.at[it, o])
            ring_pair(w, 1, 1 - w, False)

        def ring_step(w, k):
            o = (4 - k) if w == 0 else 4 + k
            if k > 1:
                arrive(("su", o), sibr_u.at[it, o])
                ring_pair(w, k, 1 - w, True)
            ring_pair(w, k, w, True)

        def own_i(oa, ob, j):
            p = cell(oa, ob)
            q = p * RT + HI * c + j
            return run_i[tab_i[q]] + sibr_i[it, ob, oa, j].astype(F32)

        def half_b():
            arrive(("shi", 2), sibr_i.at[it, 2])
            for w, ob in ((0, 1), (1, 3)):

                def one(o, carry, w=w):
                    half_s[w, o] = own_i(o, 2, w).astype(BF16)
                    return carry

                lax.fori_loop(0, 4, one, 0)
                begin(("h", w), half_s.at[w], half_r.at[it, w], {"trow": cell(0, ob)})

        def eliminate(n, carry):
            k = 2 * n
            mat = gfull[it].reshape(16, 8, TILE)
            row0 = jnp.broadcast_to(gfull[it, pl.ds(k, 1), :], (8, TILE))
            row1 = jnp.broadcast_to(gfull[it, pl.ds(k + 1, 1), :], (8, TILE))
            at0 = jnp.full((8, TILE), k, jnp.int32)

            def spread(value, at):
                return jnp.take_along_axis(value, at, axis=1, mode="promise_in_bounds")

            p = spread(row0, at0)
            q = spread(row0, at0 + 1)
            r = spread(row1, at0 + 1)
            inv_p = 1.0 / p
            t = q * inv_p
            inv_s = 1.0 / (r - q * t)
            here0 = lane8 == k
            here1 = lane8 == k + 1
            row0 = jnp.where(here0, 1.0, jnp.where(here1, 0.0, row0))
            row1 = jnp.where(here1, 1.0, jnp.where(here0, 0.0, row1))
            new1 = (row1 - t * row0) * inv_s
            new0 = row0 * inv_p - t * new1
            either = here0 | here1
            for m in range(16):
                block = mat[m]
                gfull[it, 8 * m : 8 * m + 8, :] = (
                    jnp.where(either, 0.0, block)
                    - spread(block, at0) * new0
                    - spread(block, at0 + 1) * new1
                )
            gfull[it, pl.ds(k, 1), :] = new0[0:1]
            gfull[it, pl.ds(k + 1, 1), :] = new1[0:1]
            return carry

        def invert(low, high):
            lax.fori_loop(low, high, eliminate, 0)

        def fold_b(w, ob):
            arrive(("h", w), half_r.at[it, w])
            arrive(("shi", ob), sibr_i.at[it, ob])

            def one(o, carry):
                for j in range(HI):
                    value = own_i(o, ob, j)
                    if j == w:
                        value = value + half_r[it, w, o].astype(F32)
                    full_s[w, o, j] = value.astype(BF16)
                return carry

            lax.fori_loop(0, 4, one, 0)
            for o in (2, 1, 3, 0):
                begin(
                    ("f", w, o), full_s.at[w, o], full_r.at[it, w, o], {"trow": cell(0, ob)}
                )

        def take_b(o):
            for w in range(2):
                arrive(("f", w, o), full_r.at[it, w, o])
            for j in range(HI):
                quarter[o, j] = (
                    own_i(o, 0, j) + full_r[it, 0, o, j].astype(F32) + full_r[it, 1, o, j].astype(F32)
                )

        def half_a():
            for w, oa in ((0, 1), (1, 3)):
                ah_s[w] = quarter[2, w].astype(BF16)
                begin(("ah", w), ah_s.at[w], ah_r.at[it, w], {"trow": cell(oa, 0)})

        def fold_a():
            for w, oa in ((0, 1), (1, 3)):
                arrive(("ah", w), ah_r.at[it, w])
                for j in range(HI):
                    value = quarter[oa, j]
                    if j == w:
                        value = value + ah_r[it, w].astype(F32)
                    af_s[w, j] = value.astype(BF16)
                begin(("af2", w), af_s.at[w], af_r.at[it, w], {"trow": cell(oa, 0)})

        def reduce(after_users, after_items):
            half_b()
            arrive(("su", 4), sibr_u.at[it, 4])
            ring_first(0)
            ring_first(1)
            ring_second(0)
            ring_second(1)
            await_bytes(gfull.at[it, pl.ds(0, 16 * (NZ - 1))], rsem.at[it, number("gd")])
            invert(0, 10)
            ring_step(0, 1)
            ring_step(1, 1)
            fold_b(0, 1)
            fold_b(1, 3)
            invert(10, 26)
            ring_step(0, 2)
            ring_step(1, 2)
            arrive(("shi", 0), sibr_i.at[it, 0])
            take_b(2)
            half_a()
            take_b(1)
            take_b(3)
            invert(26, 42)
            ring_step(0, 3)
            ring_step(1, 3)
            fold_a()
            take_b(0)
            invert(42, TILE // 2)
            finish(after_users, after_items)

        def finish(after_users, after_items):
            begin("inv", gfull.at[it], gother.at[it], sibling)
            arrive(("su", 0), sibr_u.at[it, 0])
            for w in range(2):
                for pr in range(2):
                    arrive(("r", w, 3, pr), ring_r.at[it, w, 3, pl.ds(2 * pr, 2)])
            grad_u = jnp.concatenate(
                [
                    own_u(0, l)
                    + sibr_u[it, 0, l].astype(F32)
                    + ring_r[it, 0, 3, l].astype(F32)
                    + ring_r[it, 1, 3, l].astype(F32)
                    for l in range(HU)
                ],
                axis=0,
            )
            arrive("inv", gother.at[it])
            inverse_i = jnp.where(c == 0, gother[it], gfull[it])
            step_u = jnp.dot(grad_u, inverse_i, precision=HIGHEST, preferred_element_type=F32)
            u_cur[...] = u_cur[...] - user_coef * step_u.reshape(HU, TILE, TILE)
            after_users()
            for w in range(2):
                arrive(("af2", w), af_r.at[it, w])
            grad_i = jnp.concatenate(
                [
                    quarter[0, j] + af_r[it, 0, j].astype(F32) + af_r[it, 1, j].astype(F32)
                    for j in range(HI)
                ],
                axis=0,
            )
            inverse_u = jnp.where(c == 0, gfull[it], gother[it])
            step_i = jnp.dot(grad_i, inverse_u, precision=HIGHEST, preferred_element_type=F32)
            i_cur[...] = i_cur[...] - item_coef * step_i.reshape(HI, TILE, TILE)
            after_items()

        def drain():
            for copy in pending:
                copy.wait_send()
            for o in range(NZ):
                await_bytes(other_u(o), ssem.at[it, number(("sg", o))])
            await_bytes(pool_i.at[it, pl.ds(0, NT // 2)], ssem.at[it, number("si")])
            await_bytes(gz.at[it], ssem.at[it, number("gz")])
            await_bytes(gxy.at[it, pl.ds(0, NXY - 1)], ssem.at[it, number("gxy")])
            await_bytes(gfull.at[it, pl.ds(0, 16 * (NZ - 1))], ssem.at[it, number("gd")])
            assert len(names) <= 128, len(names)

        return start_users, start_items, gather, terms, reduce, drain

    def send_lists():
        for d in range(1, NZ):
            remote(
                sends.at[pl.ds(0, NZ)], lists_u.at[z], lsem.at[3], lsem.at[4], {"tcol": (z + d) % NZ}
            ).start()
        for d in range(1, NXY):
            remote(
                sends.at[pl.ds(NZ, NXY)],
                lists_i.at[trow],
                lsem.at[5],
                lsem.at[6],
                {"trow": (trow + d) % NXY},
            ).start()
        lists_u[z] = sends[0:NZ, :]
        lists_i[trow] = sends[NZ : NZ + NXY, :]

    last_u = remote(u_cur, out_u.at[pl.ds(HU * c, HU)], lsem.at[1], lsem.at[7], sibling)
    last_i = remote(i_cur, out_i.at[pl.ds(HI * c, HI)], lsem.at[2], lsem.at[8], sibling)
    phases = [build(it) for it in range(ITERS)]
    phases[0][0]()
    phases[0][1]()
    send_lists()
    for it in range(ITERS):
        _, _, gather, terms, reduce, drain = phases[it]
        gather()
        terms()
        if it + 1 < ITERS:
            reduce(phases[it + 1][0], phases[it + 1][1])
        else:
            reduce(last_u.start, last_i.start)
        drain()

    for l in range(HU):
        out_u[HU * c + l] = u_cur[l]
    for l in range(HI):
        out_i[HI * c + l] = i_cur[l]
    last_u.wait()
    last_i.wait()


def write_out(new_u, new_i, out_u, out_i, sems):
    put_u = pltpu.make_async_copy(new_u, out_u, sems.at[0])
    put_i = pltpu.make_async_copy(new_i, out_i, sems.at[1])
    put_u.start()
    put_i.start()
    put_u.wait()
    put_i.wait()


def on_device(
    users, items, ratings, row_mask, col_mask, row_slots, col_slots, send_users, send_items
):
    own_users = users.shape[0] // TILE
    own_items = items.shape[0] // TILE
    all_users = own_users * TILE * NXY * NZ
    all_items = own_items * TILE * NXY * NZ
    user_coef = 2.0 * all_items * own_users / (TILE * NT * 2)
    item_coef = 2.0 * all_users * own_items / (TILE * NT * 2)
    sends = jnp.concatenate(
        [
            jnp.pad(send_users.reshape(NZ, CAPL), ((0, 0), (0, TILE - CAPL))),
            jnp.pad(send_items.reshape(NXY, CAPR), ((0, 0), (0, TILE - CAPR))),
        ],
        axis=0,
    )

    any_spec = pl.BlockSpec(memory_space=pl.ANY)
    vmem_spec = pl.BlockSpec(memory_space=pltpu.VMEM)
    square = (TILE, TILE)
    table = pltpu.SMEM((NT,), jnp.int32)
    out_u, out_i = pl.pallas_call(
        functools.partial(kernel, user_coef, item_coef),
        out_shape=(
            jax.ShapeDtypeStruct((LT,) + square, F32),
            jax.ShapeDtypeStruct((RT,) + square, F32),
        ),
        in_specs=[vmem_spec] * 5 + [any_spec] * 3,
        out_specs=(vmem_spec, vmem_spec),
        scratch_shapes=[
            pltpu.VMEM((NZ, NZ, TILE), jnp.int32),
            pltpu.VMEM((NXY, NXY, TILE), jnp.int32),
            pltpu.VMEM((NZ, TILE), jnp.int32),
            pltpu.VMEM((NXY, TILE), jnp.int32),
            pltpu.SMEM((NZ, TILE), jnp.int32),
            pltpu.SMEM((NXY, TILE), jnp.int32),
            pltpu.VMEM((8, TILE), jnp.int32),
            pltpu.SMEM((8, TILE), jnp.int32),
            table,
            table,
            table,
            table,
            table,
            pltpu.VMEM((HU,) + square, F32),
            pltpu.VMEM((HI,) + square, F32),
            pltpu.VMEM((NT,) + square, BF16),
            pltpu.VMEM((NT,) + square, BF16),
            pltpu.VMEM((ITERS, NT) + square, BF16),
            pltpu.VMEM((ITERS, NT) + square, BF16),
            pltpu.VMEM((NT,) + square, BF16),
            pltpu.VMEM((NT + 1,) + square, F32),
            pltpu.VMEM((NT + 1,) + square, F32),
            pltpu.VMEM(square, F32),
            pltpu.VMEM(square, F32),
            pltpu.VMEM((ITERS,) + square, F32),
            pltpu.VMEM((ITERS, NZ - 1, 16, TILE), F32),
            pltpu.VMEM((16, TILE), F32),
            pltpu.VMEM((ITERS, NXY, 16, TILE), F32),
            pltpu.VMEM((16, TILE), F32),
            pltpu.VMEM((ITERS,) + square, F32),
            pltpu.VMEM((ITERS,) + square, F32),
            pltpu.VMEM((NZ, HU) + square, BF16),
            pltpu.VMEM((ITERS, NZ, HU) + square, BF16),
            pltpu.VMEM((2, 4, HU) + square, BF16),
            pltpu.VMEM((ITERS, 2, 4, HU) + square, BF16),
            pltpu.VMEM((4, 4, HI) + square, BF16),
            pltpu.VMEM((ITERS, 4, 4, HI) + square, BF16),
            pltpu.VMEM((2, 4) + square, BF16),
            pltpu.VMEM((ITERS, 2, 4) + square, BF16),
            pltpu.VMEM((2, 4, HI) + square, BF16),
            pltpu.VMEM((ITERS, 2, 4, HI) + square, BF16),
            pltpu.VMEM((4, HI) + square, F32),
            pltpu.VMEM((2,) + square, BF16),
            pltpu.VMEM((ITERS, 2) + square, BF16),
            pltpu.VMEM((2, HI) + square, BF16),
            pltpu.VMEM((ITERS, 2, HI) + square, BF16),
            pltpu.SemaphoreType.DMA((ITERS, 128)),
            pltpu.SemaphoreType.DMA((ITERS, 128)),
            pltpu.SemaphoreType.DMA((10,)),
        ],
        compiler_params=pltpu.CompilerParams(
            collective_id=0, has_side_effects=True, vmem_limit_bytes=60 * 1024 * 1024
        ),
        name="scaled_gd",
    )(
        row_slots.reshape(1, NT),
        col_slots.reshape(1, NT),
        sends,
        row_mask.reshape(NT, TILE),
        col_mask.reshape(NT, TILE),
        users.reshape((LT,) + square),
        items.reshape((RT,) + square),
        ratings.reshape((NT,) + square),
    )
    out_u, out_i = pl.pallas_call(
        write_out,
        out_shape=(
            jax.ShapeDtypeStruct((LT,) + square, F32),
            jax.ShapeDtypeStruct((RT,) + square, F32),
        ),
        in_specs=[vmem_spec, vmem_spec],
        out_specs=(any_spec, any_spec),
        scratch_shapes=[pltpu.SemaphoreType.DMA((2,))],
        name="write_out",
    )(out_u, out_i)
    return out_u.reshape(users.shape), out_i.reshape(items.shape)


def solution(mesh):
    return jax.shard_map(
        on_device,
        mesh=mesh,
        in_specs=(
            P(("trow", "tcol"), None),
            P(("tcol", "trow"), None),
            P("trow", "tcol", "rep", None, None, None),
            P("trow", "tcol", "rep", None, None),
            P("trow", "tcol", "rep", None, None),
            P("trow", "tcol", "rep", None),
            P("trow", "tcol", "rep", None),
            P("trow", "tcol", "rep", None, None),
            P("trow", "tcol", "rep", None, None),
        ),
        out_specs=(P(("trow", "tcol"), None), P(("tcol", "trow"), None)),
        check_vma=False,
    )
```

```python
import functools

import jax
import jax.numpy as jnp
from jax import lax
from jax.experimental import pallas as pl
from jax.experimental.pallas import tpu as pltpu
from jax.sharding import PartitionSpec as P

ITERS = 2
TILE = 128
NX = 4
NY = 4
NZ = 8
NXY = NX * NY
LT = 8
RT = 4
NT = 64
PIVOTS = 4
CAPL = 4
CAPR = 2
HU = LT // 2
HI = RT // 2
F32 = jnp.float32
BF16 = jnp.bfloat16
HIGHEST = lax.Precision.HIGHEST


def kernel(
    user_coef,
    item_coef,
    row_slots,
    col_slots,
    send_users,
    send_items,
    row_mask,
    col_mask,
    users,
    items,
    ratings,
    out_u,
    out_i,
    sends,
    lists_u,
    lists_i,
    rows_u,
    rows_i,
    slists_u,
    slists_i,
    vtab,
    tab,
    x_row,
    y_row,
    x_col,
    tab_u,
    tab_i,
    u_cur,
    i_cur,
    rat,
    weights,
    pool_u,
    pool_i,
    errs,
    run_u,
    run_i,
    gmine,
    gsend,
    gsib,
    gz,
    gchunk,
    gxy,
    gsum,
    gfull,
    gother,
    sibs_u,
    sibr_u,
    ring_s,
    ring_r,
    sibs_i,
    sibr_i,
    half_s,
    half_r,
    full_s,
    full_r,
    quarter,
    ah_s,
    ah_r,
    af_s,
    af_r,
    ssem,
    rsem,
    lsem,
):
    trow = lax.axis_index("trow")
    z = lax.axis_index("tcol")
    c = lax.axis_index("rep")
    other = 1 - c
    x = trow // NY
    y = trow % NY
    a = jnp.where(c == 0, x, y)
    b = jnp.where(c == 0, y, x)
    sa = 4 - 3 * c
    sb = 1 + 3 * c

    def cell(oa, ob):
        return ((a + oa) % 4) * sa + ((b + ob) % 4) * sb

    def remote(src, dst, send_sem, recv_sem, where):
        return pltpu.make_async_remote_copy(
            src_ref=src,
            dst_ref=dst,
            send_sem=send_sem,
            recv_sem=recv_sem,
            device_id=where,
            device_id_type=pl.DeviceIdType.MESH,
        )

    def await_bytes(ref, sem):
        pltpu.make_async_copy(ref, ref, sem).wait()

    sibling = {"rep": other}

    sends[...] = jnp.zeros((8, TILE), jnp.int32)
    sends[0:CAPL, 0:NZ] = send_users[...]
    sends[CAPL : CAPL + CAPR, 0:NXY] = send_items[...]

    load_r = pltpu.make_async_copy(ratings, rat, lsem.at[0])
    load_u = pltpu.make_async_copy(users.at[pl.ds(HU * c, HU)], u_cur, lsem.at[1])
    load_i = pltpu.make_async_copy(items.at[pl.ds(HI * c, HI)], i_cur, lsem.at[2])
    load_u.start()
    load_i.start()
    load_r.start()

    barrier = pltpu.get_barrier_semaphore()
    for d in range(1, NZ):
        pl.semaphore_signal(
            barrier, inc=1, device_id={"tcol": (z + d) % NZ}, device_id_type=pl.DeviceIdType.MESH
        )
    for d in range(1, NXY):
        pl.semaphore_signal(
            barrier,
            inc=1,
            device_id={"trow": (trow + d) % NXY},
            device_id_type=pl.DeviceIdType.MESH,
        )
    pl.semaphore_signal(barrier, inc=1, device_id=sibling, device_id_type=pl.DeviceIdType.MESH)
    lane8 = lax.broadcasted_iota(jnp.int32, (8, TILE), 1)

    def mask_columns():
        padded = jnp.concatenate(
            [row_mask[...].astype(F32), jnp.zeros((TILE - NT, TILE), F32)], axis=0
        )
        quarter[0, 0] = padded.T

    def make_weights(low, high):
        def one(t, carry):
            spread = jnp.take_along_axis(
                quarter[0, 0], jnp.full((TILE, TILE), t, jnp.int32), axis=1, mode="promise_in_bounds"
            )
            weights[t] = (spread * col_mask[pl.ds(t, 1), :].astype(F32)).astype(BF16)
            return carry

        lax.fori_loop(low, high, one, 0, unroll=4)

    def order_tiles():
        at = lax.broadcasted_iota(jnp.int32, (NT, NT), 0).astype(F32)
        against = lax.broadcasted_iota(jnp.int32, (NT, NT), 1).astype(F32)

        def upright(row):
            return jnp.sum(jnp.where(at == against, row, 0.0), axis=1, keepdims=True)

        def order(row):
            col = upright(row)
            tied = jnp.where(row == col, jnp.where(against < at, 1.0, 0.0), 0.0)
            rank = jnp.sum(jnp.where(row < col, 1.0, tied), axis=1, keepdims=True)
            return col, rank, jnp.where(rank == against, 1.0, 0.0)

        def nearness(slot):
            o = (lax.shift_right_logical(slot, 2) + NZ - z) & (NZ - 1)
            place = jnp.where(o > 4, 2 * (NZ - o) - 1, 2 * o)
            place = jnp.where(o == 4, 7, place)
            return (CAPL * place + (slot & (CAPL - 1))).astype(F32)

        def along(placed, col):
            return jnp.sum(placed * col, axis=0, keepdims=True)

        lanes = lax.broadcasted_iota(jnp.int32, (1, NT), 1)
        row_key, row_rank, row_placed = order(nearness(row_slots[...]))
        col_col, _, col_placed = order(col_slots[...].astype(F32))
        row_col = upright(row_slots[...].astype(F32))
        row_first = jnp.sum(jnp.where(row_key < nearness(lanes), 1.0, 0.0), axis=0, keepdims=True)
        col_first = jnp.sum(jnp.where(col_col < against, 1.0, 0.0), axis=0, keepdims=True)
        table = jnp.concatenate(
            [
                along(row_placed, at[:, 0:1]),
                along(row_placed, row_col),
                along(row_placed, col_col),
                along(col_placed, row_rank),
                along(col_placed, col_col),
                along(col_placed, row_col),
                row_first,
                col_first,
            ],
            axis=0,
        )
        kind = lax.broadcasted_iota(jnp.int32, (8, TILE), 0)
        largest = jnp.where((kind == 0) | (kind == 3) | (kind > 5), NT - 1, NT // 2 - 1)
        table = jnp.concatenate([table, jnp.zeros((8, TILE - NT), F32)], axis=1)
        vtab[...] = jnp.minimum(jnp.maximum(table.astype(jnp.int32), 0), largest)
        pltpu.make_async_copy(vtab, tab, lsem.at[9]).start()

    def make_tables():
        await_bytes(lists_u.at[pl.ds(0, NZ - 1)], lsem.at[3])
        await_bytes(lists_u.at[pl.ds(0, NZ - 1)], lsem.at[4])
        await_bytes(lists_i.at[pl.ds(0, NXY - 1)], lsem.at[5])
        await_bytes(lists_i.at[pl.ds(0, NXY - 1)], lsem.at[6])
        def spread(value, at):
            return jnp.sum(jnp.where(lane8 == at, value.astype(F32), 0.0), axis=1, keepdims=True)

        gathered_u = jnp.zeros((8, TILE), F32)
        for s in range(NZ):
            gathered_u = jnp.where(lane8 == s, spread(lists_u[s], z), gathered_u)
        rows_u[...] = jnp.minimum(jnp.maximum(gathered_u.astype(jnp.int32), 0), LT - 1)
        gathered_i = jnp.zeros((8, TILE), F32)
        for s in range(NXY):
            gathered_i = jnp.where(lane8 == s, spread(lists_i[s], trow), gathered_i)
        rows_i[...] = jnp.minimum(jnp.maximum(gathered_i.astype(jnp.int32), 0), RT - 1)
        down_u = pltpu.make_async_copy(rows_u, slists_u, lsem.at[7])
        down_i = pltpu.make_async_copy(rows_i, slists_i, lsem.at[8])
        down_u.start()
        down_i.start()

    def finish_tables():
        pltpu.make_async_copy(vtab, tab, lsem.at[9]).wait()
        pltpu.make_async_copy(rows_u, slists_u, lsem.at[7]).wait()
        pltpu.make_async_copy(rows_i, slists_i, lsem.at[8]).wait()

        def user_tile(slot):
            source = slot // CAPL
            tile = source * LT + slists_u[slot % CAPL, source]
            return jnp.minimum(jnp.maximum(tile, 0), NT - 1)

        def item_tile(slot):
            source = slot // CAPR
            tile = source * RT + slists_i[CAPL + slot % CAPR, source]
            return jnp.minimum(jnp.maximum(tile, 0), NT - 1)

        def one(k, carry):
            x_row[k] = user_tile(tab[1, k])
            y_row[k] = item_tile(tab[2, k])
            x_col[k] = user_tile(tab[5, k])
            source = k // LT
            found = jnp.int32(NT)
            for s in range(CAPL):
                found = jnp.where(
                    slists_u[s, source] == k % LT, tab[6, source * CAPL + s], found
                )
            tab_u[k] = found
            source = k // RT
            found = jnp.int32(NT)
            for s in range(CAPR):
                found = jnp.where(
                    slists_i[CAPL + s, source] == k % RT,
                    tab[7, source * CAPR + s],
                    found,
                )
            tab_i[k] = found
            return carry

        lax.fori_loop(0, NT, one, 0, unroll=2)
        run_u[NT] = jnp.zeros((TILE, TILE), F32)
        run_i[NT] = jnp.zeros((TILE, TILE), F32)

    order_tiles()
    mask_columns()
    make_weights(0, NT)
    load_u.wait()
    load_i.wait()
    pl.semaphore_wait(barrier, NZ - 1 + NXY - 1 + 1)

    names = {}

    def build(it):
        pending = []

        def number(name):
            names.setdefault(name, len(names))
            return names[name]

        def begin(name, src, dst, where):
            n = number(name)
            copy = remote(src, dst, ssem.at[it, n], rsem.at[it, n], where)
            copy.start()
            pending.append(copy)

        def arrive(name, ref):
            await_bytes(ref, rsem.at[it, number(name)])

        def pair_u(o, pr):
            return pool_u.at[it, pl.ds(((z + o) % NZ) * LT + HU * c + 2 * pr, 2)]

        def send_u(way, step, pr):
            ref = pair_u(-way * (step - 1) + NZ, pr)
            begin(("u", way, step, pr), ref, ref, {"tcol": (z + way + NZ) % NZ})

        def sib_u(o, pr):
            ref = pair_u(o, pr)
            n = number(("sg", o % NZ))
            remote(ref, ref, ssem.at[it, n], rsem.at[it, n], sibling).start()

        def other_u(o):
            return pool_u.at[it, pl.ds(((z + o) % NZ) * LT + HU * other, HU)]

        def chunk_i(oa, ob):
            return pool_i.at[it, pl.ds(cell(oa, ob) * RT + HI * c, HI)]

        def tile_i(oa, ob, j):
            return pool_i.at[it, pl.ds(cell(oa, ob) * RT + HI * c + j, 1)]

        def along_a(way):
            return {"trow": cell(way + 4, 0)}

        def along_b(way):
            return {"trow": cell(0, way + 4)}

        def sib_i(oa, ob):
            ref = chunk_i(oa, ob)
            n = number("si")
            remote(ref, ref, ssem.at[it, n], rsem.at[it, n], sibling).start()

        def second_i(oa):
            for way in (1, -1):
                begin(("b", way, oa), chunk_i(oa, 0), chunk_i(oa, 0), along_b(way))

        def start_users():
            for l in range(HU):
                pool_u[it, z * LT + HU * c + l] = u_cur[l].astype(BF16)
            for pr in range(2):
                for way in (1, -1):
                    send_u(way, 1, pr)
            for pr in range(2):
                sib_u(0, pr)

        def start_items():
            for l in range(HI):
                pool_i[it, trow * RT + HI * c + l] = i_cur[l].astype(BF16)
            for way in (1, -1):
                begin(("a", way), chunk_i(0, 0), chunk_i(0, 0), along_a(way))
            second_i(0)
            sib_i(0, 0)

        def gram(ref, count):
            flat = ref[...].reshape(count * TILE, TILE)
            return lax.dot_general(
                flat, flat, (((0,), (0,)), ((), ())), precision=HIGHEST, preferred_element_type=F32
            )

        def start_gram():
            gram_u = gram(u_cur, HU)
            gram_i = gram(i_cur, HI)
            gsend[...] = jnp.where(c == 0, gram_i, gram_u)
            begin("gs", gsend, gsib.at[it], sibling)
            gmine[...] = jnp.where(c == 0, gram_u, gram_i)

        def gram_along_z():
            arrive("gs", gsib.at[it])
            gmine[...] += gsib[it]
            for d in range(1, NZ):
                zz = (z + d) % NZ
                remote(
                    gmine.at[pl.ds(16 * zz, 16)],
                    gz.at[it, d - 1],
                    ssem.at[it, number("gz")],
                    rsem.at[it, number("gz")],
                    {"tcol": zz},
                ).start()

        def gram_across():
            await_bytes(gz.at[it], rsem.at[it, number("gz")])
            total = gmine[pl.ds(16 * z, 16), :]
            for d in range(NZ - 1):
                total = total + gz[it, d]
            gchunk[...] = total
            gxy[it, trow] = total
            for d in range(1, NXY):
                remote(
                    gchunk,
                    gxy.at[it, trow],
                    ssem.at[it, number("gxy")],
                    rsem.at[it, number("gxy")],
                    {"trow": (trow + d) % NXY},
                ).start()

        def gram_whole():
            await_bytes(gxy.at[it, pl.ds(0, NXY - 1)], rsem.at[it, number("gxy")])
            total = gxy[it, 0]
            for d in range(1, NXY):
                total = total + gxy[it, d]
            gsum[...] = total
            gfull[it, pl.ds(16 * z, 16), :] = total
            for d in range(1, NZ):
                remote(
                    gsum,
                    gfull.at[it, pl.ds(16 * z, 16)],
                    ssem.at[it, number("gd")],
                    rsem.at[it, number("gd")],
                    {"tcol": (z + d) % NZ},
                ).start()

        def got_u(way, step, pr):
            arrive(("u", way, step, pr), pair_u(-way * step + NZ, pr))
            if step < 3 or (step == 3 and pr == (0 if way == 1 else 1)):
                send_u(way, step + 1, pr)
            sib_u(-way * step + NZ, pr)

        def first_got(way):
            oa = (4 - way) % 4
            arrive(("a", way), chunk_i(oa, 0))
            j = 0 if way == 1 else 1
            ref = tile_i(oa, 0, j)
            begin(("af", way), ref, ref, along_a(way))
            second_i(oa)
            sib_i(oa, 0)

        def first_far():
            for way, j in ((1, 0), (-1, 1)):
                arrive(("af", way), tile_i(2, 0, j))
            second_i(2)
            sib_i(2, 0)

        def second_got(oa):
            for way, j in ((1, 0), (-1, 1)):
                arrive(("b", way, oa), chunk_i(oa, 4 - way))
                ref = tile_i(oa, 4 - way, j)
                begin(("bf", way, oa), ref, ref, along_b(way))
                sib_i(oa, 4 - way)

        def second_far(oa):
            for way, j in ((1, 0), (-1, 1)):
                arrive(("bf", way, oa), tile_i(oa, 2, j))
            sib_i(oa, 2)

        def at_first(job):
            if it == 0:
                job()

        def error_pass(k, carry):
            t = tab[0, k]
            predicted = lax.dot_general(
                pool_u[it, x_row[k]],
                pool_i[it, y_row[k]],
                (((1,), (1,)), ((), ())),
                preferred_element_type=F32,
            )
            errs[k] = ((predicted - rat[t].astype(F32)) * weights[t].astype(F32)).astype(BF16)
            return carry

        def gather():
            start_gram()
            gram_along_z()
            for pr in range(2):
                for way in (1, -1):
                    got_u(way, 1, pr)
            first_got(1)
            first_got(-1)
            second_got(0)
            at_first(make_tables)
            first_far()
            for pr in range(2):
                for way in (1, -1):
                    got_u(way, 2, pr)
            second_got(3)
            second_got(1)
            second_far(0)
            for way in (1, -1):
                got_u(way, 3, 0)
            gram_across()
            second_got(2)
            for way in (1, -1):
                got_u(way, 3, 1)
            second_far(3)
            second_far(1)
            second_far(2)
            at_first(finish_tables)
            at_first(load_r.wait)
            arrive("si", pool_i.at[it, pl.ds(0, NT // 2)])
            got_u(1, 4, 0)
            got_u(-1, 4, 1)
            for o in range(NZ):
                arrive(("sg", o), other_u(o))
            lax.fori_loop(0, 16, error_pass, 0, unroll=8)
            gram_whole()
            lax.fori_loop(16, NT, error_pass, 0, unroll=8)

        zero = jnp.zeros((TILE, TILE), F32)

        def item_pass(n, carry):
            k = NT - 1 - n
            run, before = carry
            slot = tab[4, k]
            term = lax.dot_general(
                errs[tab[3, k]],
                pool_u[it, x_col[k]],
                (((0,), (0,)), ((), ())),
                preferred_element_type=F32,
            )
            run = jnp.where(slot == before, run, 0.0) + term
            run_i[k] = run
            return run, slot

        def share_i(ob):
            def one(oa, carry, ob=ob):
                p = ((b + oa) % 4) * sb + ((a + ob) % 4) * sa
                q = p * RT + HI * other
                for j in range(HI):
                    sibs_i[ob, oa, j] = run_i[tab_i[q + j]].astype(BF16)
                return carry

            lax.fori_loop(0, 4, one, 0)
            begin(("shi", ob), sibs_i.at[ob], sibr_i.at[it, ob], sibling)

        def user_pass(n, carry):
            k = NT - 1 - n
            run, before = carry
            slot = tab[1, k]
            term = jnp.dot(errs[k], pool_i[it, y_row[k]], preferred_element_type=F32)
            run = jnp.where(slot == before, run, 0.0) + term
            run_u[k] = run
            return run, slot

        def terms():
            lax.fori_loop(0, NT, item_pass, (zero, jnp.int32(-1)), unroll=8)
            for ob in (2, 1, 3, 0):
                share_i(ob)
            carry = lax.fori_loop(0, 36, user_pass, (zero, jnp.int32(-1)), unroll=9)
            share_u(4)
            for n, o in enumerate((3, 5, 2, 6, 1, 7, 0)):
                carry = lax.fori_loop(36 + 4 * n, 40 + 4 * n, user_pass, carry, unroll=4)
                share_u(o)

        def own_u(o, l):
            p = ((z + o) % NZ) * LT + HU * c + l
            return run_u[tab_u[p]]

        def share_u(o):
            def one(l, carry):
                p = ((z + o) % NZ) * LT + HU * other + l
                sibs_u[o, l] = run_u[tab_u[p]].astype(BF16)
                return carry

            lax.fori_loop(0, HU, one, 0)
            begin(("su", o), sibs_u.at[o], sibr_u.at[it, o], sibling)

        def ring_send(w, k, pr):
            ref = ring_s.at[w, k, pl.ds(2 * pr, 2)]
            begin(
                ("r", w, k, pr),
                ref,
                ring_r.at[it, w, k, pl.ds(2 * pr, 2)],
                {"tcol": (z + (1, NZ - 1)[w]) % NZ},
            )

        def ring_first(w):
            for l in (2 * w, 2 * w + 1):
                ring_s[w, 0, l] = (own_u(4, l) + sibr_u[it, 4, l].astype(F32)).astype(BF16)
            ring_send(w, 0, w)

        def ring_pair(w, k, pr, held):
            o = (4 - k) if w == 0 else 4 + k
            if held:
                arrive(("r", w, k - 1, pr), ring_r.at[it, w, k - 1, pl.ds(2 * pr, 2)])
            for l in (2 * pr, 2 * pr + 1):
                value = own_u(o, l) + sibr_u[it, o, l].astype(F32)
                if held:
                    value = value + ring_r[it, w, k - 1, l].astype(F32)
                ring_s[w, k, l] = value.astype(BF16)
            ring_send(w, k, pr)

        def ring_second(w):
            o = (3, 5)[w]
            arrive(("su", o), sibr_u.at[it, o])
            ring_pair(w, 1, 1 - w, False)

        def ring_step(w, k):
            o = (4 - k) if w == 0 else 4 + k
            if k > 1:
                arrive(("su", o), sibr_u.at[it, o])
                ring_pair(w, k, 1 - w, True)
            ring_pair(w, k, w, True)

        def own_i(oa, ob, j):
            p = cell(oa, ob)
            q = p * RT + HI * c + j
            return run_i[tab_i[q]] + sibr_i[it, ob, oa, j].astype(F32)

        def half_b():
            arrive(("shi", 2), sibr_i.at[it, 2])
            for w, ob in ((0, 1), (1, 3)):

                def one(o, carry, w=w):
                    half_s[w, o] = own_i(o, 2, w).astype(BF16)
                    return carry

                lax.fori_loop(0, 4, one, 0)
                begin(("h", w), half_s.at[w], half_r.at[it, w], {"trow": cell(0, ob)})

        def eliminate(n, carry):
            k = PIVOTS * n
            mat = gfull[it].reshape(16, 8, TILE)
            at = [jnp.full((8, TILE), k + j, jnp.int32) for j in range(PIVOTS)]

            def spread(value, j):
                return jnp.take_along_axis(value, at[j], axis=1, mode="promise_in_bounds")

            rows = [
                jnp.broadcast_to(gfull[it, pl.ds(k + i, 1), :], (8, TILE)) for i in range(PIVOTS)
            ]
            core = [
                [spread(rows[i], j) if j >= i else None for j in range(PIVOTS)]
                for i in range(PIVOTS)
            ]
            for i in range(PIVOTS):
                for j in range(i):
                    core[i][j] = core[j][i]
            inside = (lane8 >= k) & (lane8 < k + PIVOTS)
            rows = [
                jnp.where(lane8 == k + i, 1.0, jnp.where(inside, 0.0, rows[i]))
                for i in range(PIVOTS)
            ]
            for i in range(PIVOTS):
                scale = 1.0 / core[i][i]
                rows[i] = rows[i] * scale
                for j in range(i + 1, PIVOTS):
                    core[i][j] = core[i][j] * scale
                for m in range(PIVOTS):
                    if m != i:
                        for j in range(i + 1, PIVOTS):
                            core[m][j] = core[m][j] - core[m][i] * core[i][j]
                        rows[m] = rows[m] - core[m][i] * rows[i]
            for m in range(16):
                block = mat[m]
                value = jnp.where(inside, 0.0, block)
                for j in range(PIVOTS):
                    value = value - spread(block, j) * rows[j]
                gfull[it, 8 * m : 8 * m + 8, :] = value
            for i in range(PIVOTS):
                gfull[it, pl.ds(k + i, 1), :] = rows[i][0:1]
            return carry

        def invert(low, high):
            lax.fori_loop(low, high, eliminate, 0)

        def fold_b(w, ob):
            arrive(("h", w), half_r.at[it, w])
            arrive(("shi", ob), sibr_i.at[it, ob])

            def one(o, carry):
                for j in range(HI):
                    value = own_i(o, ob, j)
                    if j == w:
                        value = value + half_r[it, w, o].astype(F32)
                    full_s[w, o, j] = value.astype(BF16)
                return carry

            lax.fori_loop(0, 4, one, 0)
            for o in (2, 1, 3, 0):
                begin(
                    ("f", w, o), full_s.at[w, o], full_r.at[it, w, o], {"trow": cell(0, ob)}
                )

        def take_b(o):
            for w in range(2):
                arrive(("f", w, o), full_r.at[it, w, o])
            for j in range(HI):
                quarter[o, j] = (
                    own_i(o, 0, j) + full_r[it, 0, o, j].astype(F32) + full_r[it, 1, o, j].astype(F32)
                )

        def half_a():
            for w, oa in ((0, 1), (1, 3)):
                ah_s[w] = quarter[2, w]
                begin(("ah", w), ah_s.at[w], ah_r.at[it, w], {"trow": cell(oa, 0)})

        def fold_a():
            for w, oa in ((0, 1), (1, 3)):
                arrive(("ah", w), ah_r.at[it, w])
                for j in range(HI):
                    value = quarter[oa, j]
                    if j == w:
                        value = value + ah_r[it, w]
                    af_s[w, j] = value
                begin(("af2", w), af_s.at[w], af_r.at[it, w], {"trow": cell(oa, 0)})

        def reduce(after_users, after_items):
            half_b()
            arrive(("su", 4), sibr_u.at[it, 4])
            ring_first(0)
            ring_first(1)
            ring_second(0)
            ring_second(1)
            await_bytes(gfull.at[it, pl.ds(0, 16 * (NZ - 1))], rsem.at[it, number("gd")])
            invert(0, 5)
            ring_step(0, 1)
            ring_step(1, 1)
            fold_b(0, 1)
            fold_b(1, 3)
            invert(5, 13)
            ring_step(0, 2)
            ring_step(1, 2)
            arrive(("shi", 0), sibr_i.at[it, 0])
            take_b(2)
            half_a()
            take_b(1)
            take_b(3)
            invert(13, 21)
            ring_step(0, 3)
            ring_step(1, 3)
            fold_a()
            take_b(0)
            invert(21, TILE // PIVOTS)
            finish(after_users, after_items)

        def finish(after_users, after_items):
            begin("inv", gfull.at[it], gother.at[it], sibling)
            arrive(("su", 0), sibr_u.at[it, 0])
            for w in range(2):
                for pr in range(2):
                    arrive(("r", w, 3, pr), ring_r.at[it, w, 3, pl.ds(2 * pr, 2)])
            grad_u = jnp.concatenate(
                [
                    own_u(0, l)
                    + sibr_u[it, 0, l].astype(F32)
                    + ring_r[it, 0, 3, l].astype(F32)
                    + ring_r[it, 1, 3, l].astype(F32)
                    for l in range(HU)
                ],
                axis=0,
            )
            arrive("inv", gother.at[it])
            inverse_i = jnp.where(c == 0, gother[it], gfull[it])
            step_u = jnp.dot(grad_u, inverse_i, precision=HIGHEST, preferred_element_type=F32)
            u_cur[...] = u_cur[...] - user_coef * step_u.reshape(HU, TILE, TILE)
            after_users()
            for w in range(2):
                arrive(("af2", w), af_r.at[it, w])
            grad_i = jnp.concatenate(
                [
                    quarter[0, j] + af_r[it, 0, j] + af_r[it, 1, j]
                    for j in range(HI)
                ],
                axis=0,
            )
            inverse_u = jnp.where(c == 0, gfull[it], gother[it])
            step_i = jnp.dot(grad_i, inverse_u, precision=HIGHEST, preferred_element_type=F32)
            i_cur[...] = i_cur[...] - item_coef * step_i.reshape(HI, TILE, TILE)
            after_items()

        def drain():
            for copy in pending:
                copy.wait_send()
            for o in range(NZ):
                await_bytes(other_u(o), ssem.at[it, number(("sg", o))])
            await_bytes(pool_i.at[it, pl.ds(0, NT // 2)], ssem.at[it, number("si")])
            await_bytes(gz.at[it], ssem.at[it, number("gz")])
            await_bytes(gxy.at[it, pl.ds(0, NXY - 1)], ssem.at[it, number("gxy")])
            await_bytes(gfull.at[it, pl.ds(0, 16 * (NZ - 1))], ssem.at[it, number("gd")])
            assert len(names) <= 128, len(names)

        return start_users, start_items, gather, terms, reduce, drain

    def send_lists():
        for d in range(1, NZ):
            remote(
                sends, lists_u.at[z], lsem.at[3], lsem.at[4], {"tcol": (z + d) % NZ}
            ).start()
        for d in range(1, NXY):
            remote(
                sends,
                lists_i.at[trow],
                lsem.at[5],
                lsem.at[6],
                {"trow": (trow + d) % NXY},
            ).start()
        lists_u[z] = sends[...]
        lists_i[trow] = sends[...]

    last_u = remote(u_cur, out_u.at[pl.ds(HU * c, HU)], lsem.at[1], lsem.at[7], sibling)
    last_i = remote(i_cur, out_i.at[pl.ds(HI * c, HI)], lsem.at[2], lsem.at[8], sibling)
    phases = [build(it) for it in range(ITERS)]
    phases[0][0]()
    phases[0][1]()
    send_lists()
    for it in range(ITERS):
        _, _, gather, terms, reduce, drain = phases[it]
        gather()
        terms()
        if it + 1 < ITERS:
            reduce(phases[it + 1][0], phases[it + 1][1])
        else:
            reduce(last_u.start, last_i.start)
        drain()

    for l in range(HU):
        out_u[HU * c + l] = u_cur[l]
    for l in range(HI):
        out_i[HI * c + l] = i_cur[l]
    last_u.wait()
    last_i.wait()


def write_out(new_u, new_i, out_u, out_i, sems):
    put_u = pltpu.make_async_copy(new_u, out_u, sems.at[0])
    put_i = pltpu.make_async_copy(new_i, out_i, sems.at[1])
    put_u.start()
    put_i.start()
    put_u.wait()
    put_i.wait()


def on_device(
    users, items, ratings, row_mask, col_mask, row_slots, col_slots, send_users, send_items
):
    own_users = users.shape[0] // TILE
    own_items = items.shape[0] // TILE
    all_users = own_users * TILE * NXY * NZ
    all_items = own_items * TILE * NXY * NZ
    user_coef = 2.0 * all_items * own_users / (TILE * NT * 2)
    item_coef = 2.0 * all_users * own_items / (TILE * NT * 2)
    any_spec = pl.BlockSpec(memory_space=pl.ANY)
    vmem_spec = pl.BlockSpec(memory_space=pltpu.VMEM)
    square = (TILE, TILE)
    table = pltpu.SMEM((NT,), jnp.int32)
    out_u, out_i = pl.pallas_call(
        functools.partial(kernel, user_coef, item_coef),
        out_shape=(
            jax.ShapeDtypeStruct((LT,) + square, F32),
            jax.ShapeDtypeStruct((RT,) + square, F32),
        ),
        in_specs=[vmem_spec] * 6 + [any_spec] * 3,
        out_specs=(vmem_spec, vmem_spec),
        scratch_shapes=[
            pltpu.VMEM((8, TILE), jnp.int32),
            pltpu.VMEM((NZ, 8, TILE), jnp.int32),
            pltpu.VMEM((NXY, 8, TILE), jnp.int32),
            pltpu.VMEM((8, TILE), jnp.int32),
            pltpu.VMEM((8, TILE), jnp.int32),
            pltpu.SMEM((8, TILE), jnp.int32),
            pltpu.SMEM((8, TILE), jnp.int32),
            pltpu.VMEM((8, TILE), jnp.int32),
            pltpu.SMEM((8, TILE), jnp.int32),
            table,
            table,
            table,
            table,
            table,
            pltpu.VMEM((HU,) + square, F32),
            pltpu.VMEM((HI,) + square, F32),
            pltpu.VMEM((NT,) + square, BF16),
            pltpu.VMEM((NT,) + square, BF16),
            pltpu.VMEM((ITERS, NT) + square, BF16),
            pltpu.VMEM((ITERS, NT) + square, BF16),
            pltpu.VMEM((NT,) + square, BF16),
            pltpu.VMEM((NT + 1,) + square, F32),
            pltpu.VMEM((NT + 1,) + square, F32),
            pltpu.VMEM(square, F32),
            pltpu.VMEM(square, F32),
            pltpu.VMEM((ITERS,) + square, F32),
            pltpu.VMEM((ITERS, NZ - 1, 16, TILE), F32),
            pltpu.VMEM((16, TILE), F32),
            pltpu.VMEM((ITERS, NXY, 16, TILE), F32),
            pltpu.VMEM((16, TILE), F32),
            pltpu.VMEM((ITERS,) + square, F32),
            pltpu.VMEM((ITERS,) + square, F32),
            pltpu.VMEM((NZ, HU) + square, BF16),
            pltpu.VMEM((ITERS, NZ, HU) + square, BF16),
            pltpu.VMEM((2, 4, HU) + square, BF16),
            pltpu.VMEM((ITERS, 2, 4, HU) + square, BF16),
            pltpu.VMEM((4, 4, HI) + square, BF16),
            pltpu.VMEM((ITERS, 4, 4, HI) + square, BF16),
            pltpu.VMEM((2, 4) + square, BF16),
            pltpu.VMEM((ITERS, 2, 4) + square, BF16),
            pltpu.VMEM((2, 4, HI) + square, BF16),
            pltpu.VMEM((ITERS, 2, 4, HI) + square, BF16),
            pltpu.VMEM((4, HI) + square, F32),
            pltpu.VMEM((2,) + square, F32),
            pltpu.VMEM((ITERS, 2) + square, F32),
            pltpu.VMEM((2, HI) + square, F32),
            pltpu.VMEM((ITERS, 2, HI) + square, F32),
            pltpu.SemaphoreType.DMA((ITERS, 128)),
            pltpu.SemaphoreType.DMA((ITERS, 128)),
            pltpu.SemaphoreType.DMA((10,)),
        ],
        compiler_params=pltpu.CompilerParams(
            collective_id=0, has_side_effects=True, vmem_limit_bytes=60 * 1024 * 1024
        ),
        name="scaled_gd",
    )(
        row_slots.reshape(1, NT),
        col_slots.reshape(1, NT),
        send_users.reshape(NZ, CAPL).T,
        send_items.reshape(NXY, CAPR).T,
        row_mask.reshape(NT, TILE),
        col_mask.reshape(NT, TILE),
        users.reshape((LT,) + square),
        items.reshape((RT,) + square),
        ratings.reshape((NT,) + square),
    )
    out_u, out_i = pl.pallas_call(
        write_out,
        out_shape=(
            jax.ShapeDtypeStruct((LT,) + square, F32),
            jax.ShapeDtypeStruct((RT,) + square, F32),
        ),
        in_specs=[vmem_spec, vmem_spec],
        out_specs=(any_spec, any_spec),
        scratch_shapes=[pltpu.SemaphoreType.DMA((2,))],
        name="write_out",
    )(out_u, out_i)
    return out_u.reshape(users.shape), out_i.reshape(items.shape)


def solution(mesh):
    return jax.shard_map(
        on_device,
        mesh=mesh,
        in_specs=(
            P(("trow", "tcol"), None),
            P(("tcol", "trow"), None),
            P("trow", "tcol", "rep", None, None, None),
            P("trow", "tcol", "rep", None, None),
            P("trow", "tcol", "rep", None, None),
            P("trow", "tcol", "rep", None),
            P("trow", "tcol", "rep", None),
            P("trow", "tcol", "rep", None, None),
            P("trow", "tcol", "rep", None, None),
        ),
        out_specs=(P(("trow", "tcol"), None), P(("tcol", "trow"), None)),
        check_vma=False,
    )
```
